128 devices in a mesh: grp: 4 (over y), row: 32 (over x, z, core).
Axes of the slice: x: 4, y: 4, z: 4, core: 2. Of those that a mesh axis runs over, the one named last changes fastest.
Arguments:
- site_blocks: float32 [32, 4, 512, 256], P('grp', None, 'row'), may hold values from -40 to 40
- row_lengths: int32 [32], replicated, may hold values from 1 to 512, 8192 in all
- column_lengths: int32 [32], replicated, may hold values from 1 to 256, 4096 in all
- joining: int32 [32, 4], replicated, may hold values from 0 to 31, as said below
- owner_slots: int32 [32], replicated, may hold values from 0 to 31, each once
- next_blocks: float32 [32, 1024, 256], P('grp', 'row'), may hold values from -90 to 90
Outputs:
- canonical: float32 [32, 4, 512, 256], P('grp', None, 'row')
- next_site: float32 [32, 1024, 256], P('grp', 'row')
The draws below stay inside these ranges and needn't reach their ends.
Inputs may be any that keep to these rules, and one draw needn't show every extreme that they name: `joining`: for each physical state, every joined sector is named by exactly one left sector. `owner_slots`: each joined sector is held in exactly one slot. `row_lengths`: one left sector has all 512 rows live.
All inputs are finite; a program needn't handle non-finite values.
Results may differ from the reference program's by a relative error of at most 0.00009.
Values sent between devices are 32-bit elements; how exact they have to be, the bound alone decides.
No kernel may reach another device: no remote copies, remote signals or barrier semaphores. Data moves between devices by JAX's collectives and lax.ppermute only.
A program may use at most 128 MiB of HBM per device.

```python
import math
import jax
import jax.numpy as jnp
import numpy as np
from jax import lax

SEC_GRP = 8
SECTORS = 32
PHYS = 4
LCAP = 512
KCAP = 256
NCOL = 1024


def draw_site_blocks(key, part):
    first_key, second_key = jax.random.split(jax.random.fold_in(key, 11))
    shape = (SECTORS, PHYS, LCAP, KCAP)
    values = jnp.clip(jax.random.normal(first_key, shape, jnp.float32), -4.0, 4.0)
    spread = jnp.exp(jax.random.uniform(second_key, (SECTORS, PHYS, LCAP, 1), jnp.float32) * math.log(10.0))
    return jnp.clip(values * spread, -40.0, 40.0).astype(jnp.float32)


def draw_joining(key, part):
    charges = jax.random.permutation(jax.random.fold_in(key, 23), SECTORS).astype(jnp.int32)
    inverse_order = jnp.argsort(charges, stable=True).astype(jnp.int32)
    numbers = jnp.array([0, 1, 1, 2], dtype=jnp.int32)
    target = (charges[:, None] + numbers[None, :]) % SECTORS
    return inverse_order[target].astype(jnp.int32)


def draw_next_blocks(key, part):
    first_key, second_key = jax.random.split(jax.random.fold_in(key, 37))
    shape = (SECTORS, NCOL, KCAP)
    groups = SECTORS // SEC_GRP
    slot_ids = (jnp.arange(SECTORS, dtype=jnp.int32) // SEC_GRP).astype(jnp.float32)[:, None, None]
    col_ids = jnp.arange(NCOL, dtype=jnp.int32).astype(jnp.float32)[None, :, None]
    fraction = (slot_ids + col_ids / NCOL) / groups
    rising = jnp.exp(fraction * math.log(3.0))
    values = jnp.clip(jax.random.normal(first_key, shape, jnp.float32), -3.0, 3.0)
    spread = jnp.exp(jax.random.uniform(second_key, (SECTORS, NCOL, 1), jnp.float32) * math.log(10.0))
    return jnp.clip(values * spread * rising, -90.0, 90.0).astype(jnp.float32)


def split_up(number_of, total, limit, slope):
    weights = [(1 << 20) // math.isqrt(standing ** slope) + 1 for standing in range(2, number_of + 1)]
    surplus, counts = total - limit - (number_of - 1), [1] * (number_of - 1)
    while surplus > 0:
        candidates = [i for i in range(number_of - 1) if counts[i] < limit]
        whole, left = sum([weights[i] for i in candidates]), surplus
        for i in candidates:
            addition = min(limit - counts[i], max(1, left * weights[i] // whole), surplus)
            counts[i] = counts[i] + addition
            surplus = surplus - addition
    return np.array([limit] + counts)


def ragged(rng, amount, total, reach, skew):
    if amount == 2:
        one = jax.random.randint(rng, (), max(1, total - reach), min(reach, total - 1) + 1)
        return jnp.stack([one, total - one])
    lengths = jnp.asarray(split_up(amount, total, reach, skew), jnp.int32)
    pairs = (amount - 1) // 2
    donor, sink = lengths[1:1 + 2 * pairs:2], lengths[2:2 + 2 * pairs:2]
    margin = jnp.minimum(donor - 1, reach - sink)
    passed = jax.random.randint(jax.random.fold_in(rng, 1), (pairs,), 0, 1 << 20) % (margin + 1)
    lengths = lengths.at[1:1 + 2 * pairs:2].set(donor - passed).at[2:2 + 2 * pairs:2].set(sink + passed)
    return lengths[jax.random.permutation(jax.random.fold_in(rng, 2), amount)]


def setup_inputs(seed: int = 0) -> dict:
    streams_of = jax.random.split(jax.random.key(seed), 7)
    site_blocks = draw_site_blocks(jax.random.fold_in(streams_of[6], 71), 0)
    row_lengths = ragged(streams_of[1], SECTORS, SECTORS * LCAP // 2, LCAP, 1).astype(jnp.int32)
    column_lengths = ragged(streams_of[2], SECTORS, SECTORS * KCAP // 2, KCAP, 1).astype(jnp.int32)
    joining = draw_joining(jax.random.fold_in(streams_of[6], 71), 0)
    owner_slots = jax.random.permutation(streams_of[4], SECTORS).astype(jnp.int32)
    next_blocks = draw_next_blocks(jax.random.fold_in(streams_of[6], 71), 0)
    return dict(site_blocks=site_blocks, row_lengths=row_lengths, column_lengths=column_lengths, joining=joining, owner_slots=owner_slots, next_blocks=next_blocks)


PRECISE = lax.Precision.HIGHEST

def reference(site_blocks, row_lengths, column_lengths, joining, owner_slots, next_blocks):
    sectors = jnp.arange(SECTORS, dtype=jnp.int32)
    columns = jnp.arange(KCAP, dtype=jnp.int32)
    row_ids = jnp.arange(LCAP, dtype=jnp.int32)
    joined_hot = joining[:, :, None] == sectors[None, None, :]
    joined_rows = lax.optimization_barrier(jnp.sum(jnp.where(joined_hot, row_lengths[:, None, None], 0), axis=(0, 1))).astype(jnp.int32)
    live_cols = jnp.minimum(column_lengths, joined_rows // 2).astype(jnp.int32)
    piece_cols = lax.optimization_barrier(jnp.sum(jnp.where(joined_hot, live_cols[None, None, :], 0), axis=2))
    row_mask = (row_ids[None, :] < row_lengths[:, None]).astype(jnp.float32)
    col_mask = (columns[None, None, :] < piece_cols[:, :, None]).astype(jnp.float32)
    masked = site_blocks * row_mask[:, None, :, None] * col_mask[:, :, None, :]
    hot_float = joined_hot.astype(jnp.float32)
    pieces = jnp.einsum('psrk,psrl->pskl', masked, masked, precision=PRECISE)
    gram_total = jnp.einsum('psq,pskl->qkl', hot_float, pieces, precision=PRECISE)
    identity = jnp.eye(KCAP, dtype=jnp.float32)
    dead_cols = (columns[None, :] >= live_cols[:, None]).astype(jnp.float32)
    gram_total = gram_total + dead_cols[:, :, None] * identity[None]
    upper_factor = jnp.swapaxes(jnp.linalg.cholesky(gram_total), 1, 2)
    inverse = lax.linalg.triangular_solve(upper_factor, jnp.broadcast_to(identity, upper_factor.shape), left_side=True, lower=False)
    inverse_picked = jnp.einsum('psq,qkl->pskl', hot_float, inverse, precision=PRECISE)
    canonical = math.sqrt(PHYS * LCAP) * jnp.einsum('psrk,pskl->psrl', masked, inverse_picked, precision=PRECISE)
    slot_hot = owner_slots[:, None] == sectors[None, :]
    slot_live = lax.optimization_barrier(jnp.sum(jnp.where(slot_hot, live_cols[None, :], 0), axis=1))
    upper_picked = jnp.einsum('pq,qkl->pkl', slot_hot.astype(jnp.float32), upper_factor, precision=PRECISE)
    next_mask = (columns[None, :] < slot_live[:, None]).astype(jnp.float32)
    masked_next = next_blocks * next_mask[:, None, :]
    absorbed = jnp.einsum('pcj,pkj->pck', masked_next, upper_picked, precision=PRECISE)
    mean_square = jnp.sum(absorbed * absorbed) / (SECTORS * NCOL * KCAP)
    next_site = absorbed * lax.rsqrt(mean_square + 1e-06)
    return (canonical, next_site)
```

```python
import functools
import math

import jax
import jax.numpy as jnp
from jax import lax
from jax.experimental import pallas as pl
from jax.experimental.pallas import tpu as pltpu
from jax.sharding import PartitionSpec as P

PRECISE = lax.Precision.HIGHEST
HALF = 128
STEP = 8
SLOT = 8
HBM = pl.BlockSpec(memory_space=pltpu.HBM)
PARAMS = pltpu.CompilerParams(vmem_limit_bytes=16 * 1024 * 1024)
VMEM = pl.BlockSpec(memory_space=pltpu.VMEM)
SMEM = pl.BlockSpec(memory_space=pltpu.SMEM)


def dot(a, b, ca, cb):
    return lax.dot_general(
        a, b, (((ca,), (cb,)), ((), ())), precision=PRECISE, preferred_element_type=jnp.float32
    )


def live_count(join_row, rows_row, column_lengths, sector):
    joined = jnp.where(join_row[...] == sector, rows_row[...], 0.0)
    joined = jnp.sum(joined, axis=1, keepdims=True)
    return jnp.minimum(jnp.floor(joined * 0.5), column_lengths[sector].astype(jnp.float32))


def gather_kernel(site_ref, next_ref, out_ref, sems):
    here = site_ref.shape[1]
    one = pltpu.make_async_copy(site_ref, out_ref.at[:, :here, :], sems.at[0])
    two = pltpu.make_async_copy(next_ref, out_ref.at[:, here:, :], sems.at[1])
    one.start()
    two.start()
    one.wait()
    two.wait()


def scatter_kernel(data_ref, site_ref, next_ref, sems):
    here = site_ref.shape[1]
    one = pltpu.make_async_copy(data_ref.at[:, :here, :], site_ref, sems.at[0])
    two = pltpu.make_async_copy(data_ref.at[:, here:, :], next_ref, sems.at[1])
    one.start()
    two.start()
    one.wait()
    two.wait()


def slot_rows(index):
    return pl.ds(index, HALF, stride=SLOT)


def gram_kernel(meta, column_lengths, join_row, rows_row, unused_one, unused_two, data_ref, out_ref):
    peers, depth, breadth = data_ref.shape
    here = depth - STEP
    site = data_ref[:, :here, :].reshape(peers * here, breadth)
    row_ids = lax.broadcasted_iota(jnp.int32, site.shape, 0)
    site = jnp.where(row_ids < meta[0], site, 0.0)
    nxt = data_ref[:, here:, :].reshape(peers * STEP, breadth)
    live_slot = live_count(join_row, rows_row, column_lengths, meta[2])
    column_ids = lax.broadcasted_iota(jnp.int32, (1, breadth), 1).astype(jnp.float32)
    nxt = jnp.where(column_ids < live_slot, nxt, 0.0)
    for start, block in ((0, site), (3, nxt)):
        top = dot(block[:, :HALF], block, 0, 0)
        out_ref[slot_rows(start), :] = top[:, :HALF]
        out_ref[slot_rows(start + 1), :] = top[:, HALF:]
        out_ref[slot_rows(start + 2), :] = dot(block[:, HALF:], block[:, HALF:], 0, 0)


def combine_kernel(join_row, join_col, owner_col, piece_ref, out_ref):
    piece = jnp.concatenate([piece_ref[slot_rows(i), :] for i in range(3)], axis=1)
    pair_hot = (join_col[...] == join_row[...]).astype(jnp.float32)
    slot_hot = (owner_col[...] == join_row[...]).astype(jnp.float32)
    pair_part = dot(pair_hot, piece, 1, 0)
    slot_part = dot(slot_hot, piece, 1, 0)
    norm = 0.0
    for i in range(3):
        cut = slice(i * HALF, (i + 1) * HALF)
        out_ref[slot_rows(i), :] = pair_part[:, cut]
        out_ref[slot_rows(3 + i), :] = slot_part[:, cut]
        weight = 2.0 if i == 1 else 1.0
        norm = norm + weight * slot_part[:, cut] * piece_ref[slot_rows(3 + i), :]
    norm = jnp.sum(jnp.sum(norm, axis=0, keepdims=True), axis=1, keepdims=True)
    out_ref[slot_rows(6), :] = jnp.broadcast_to(norm, (HALF, HALF))


def eliminate(work_ref, block):
    start = block * STEP
    shape = (STEP, HALF)
    rows = work_ref[start : start + STEP, :]
    left = [jnp.broadcast_to(rows[i : i + 1, :HALF], shape) for i in range(STEP)]
    right = [jnp.broadcast_to(rows[i : i + 1, HALF:], shape) for i in range(STEP)]
    lanes = [jnp.broadcast_to(rows[:, start + j : start + j + 1], shape) for j in range(STEP)]
    a = [[jnp.broadcast_to(lanes[j][i : i + 1, :], shape) for i in range(j + 1)] for j in range(STEP)]
    for k in range(STEP):
        root = lax.rsqrt(a[k][k])
        left[k] = left[k] * root
        right[k] = right[k] * root
        for j in range(k + 1, STEP):
            a[j][k] = a[j][k] * root
        for j in range(k + 1, STEP):
            for i in range(k + 1, j + 1):
                a[j][i] = a[j][i] - a[j][k] * a[i][k]
            left[j] = left[j] - a[j][k] * left[k]
            right[j] = right[j] - a[j][k] * right[k]
    sub = lax.broadcasted_iota(jnp.int32, shape, 0)
    lane = lax.broadcasted_iota(jnp.int32, shape, 1)
    one, two = left[0], right[0]
    for k in range(1, STEP):
        one = jnp.where(sub == k, left[k], one)
        two = jnp.where(sub == k, right[k], two)
    one = jnp.where(lane >= sub + start, one, 0.0)
    panel = jnp.concatenate([one, two], axis=1)
    work_ref[start : start + STEP, :] = panel
    if start + STEP < HALF:
        high = panel.astype(jnp.bfloat16).astype(jnp.float32)
        rest = panel - high
        middle = rest.astype(jnp.bfloat16).astype(jnp.float32)
        low = rest - middle
        lhs = jnp.concatenate([high, high, middle, middle, high, low], axis=0)[:, :HALF]
        rhs = jnp.concatenate([high, middle, high, middle, low, high], axis=0)
        update = lax.dot_general(
            lhs.astype(jnp.bfloat16),
            rhs.astype(jnp.bfloat16),
            (((0,), (0,)), ((), ())),
            preferred_element_type=jnp.float32,
        )
        work_ref[start + STEP :, :] = work_ref[start + STEP :, :] - update[start + STEP :, :]


def apply_kernel(
    entries, meta, column_lengths, join_row, rows_row, data_ref, gram_ref, out_ref, first, second, kept
):
    peers, depth, breadth = data_ref.shape
    here = depth - STEP
    live_pair = live_count(join_row, rows_row, column_lengths, meta[1])
    live_slot = live_count(join_row, rows_row, column_lengths, meta[2])
    sub = lax.broadcasted_iota(jnp.int32, (HALF, HALF), 0)
    lane = lax.broadcasted_iota(jnp.int32, (HALF, HALF), 1)
    eye = jnp.where(sub == lane, 1.0, 0.0)
    sub = sub.astype(jnp.float32)
    lane = lane.astype(jnp.float32)

    def masked(start, live, row_from, col_from):
        block = gram_ref[slot_rows(start), :]
        alive = jnp.logical_and(sub + row_from < live, lane + col_from < live)
        return jnp.where(alive, block, eye if row_from == col_from else 0.0)

    first[:, :HALF] = masked(0, live_pair, 0, 0)
    first[:, HALF:] = eye
    second[:, :HALF] = masked(3, live_slot, 0, 0)
    second[:, HALF:] = masked(4, live_slot, 0, HALF)

    def half(index, carry):
        for block in range(HALF // STEP):
            eliminate(first, block)
            eliminate(second, block)

        @pl.when(index == 0)
        def _():
            pair_turn = first[:, HALF:]
            pair_cross = dot(pair_turn, masked(1, live_pair, 0, HALF), 1, 0)
            slot_cross = second[:, HALF:]
            kept[:, :HALF] = pair_turn
            kept[:, HALF : 2 * HALF] = pair_cross
            kept[:, 2 * HALF : 4 * HALF] = second[...]
            first[:, :HALF] = masked(2, live_pair, HALF, HALF) - dot(
                pair_cross, pair_cross, 0, 0
            )
            first[:, HALF:] = eye
            second[:, :HALF] = masked(5, live_slot, HALF, HALF) - dot(
                slot_cross, slot_cross, 0, 0
            )

        return carry

    lax.fori_loop(0, 2, half, 0)

    column_ids = lax.broadcasted_iota(jnp.int32, (1, breadth), 1).astype(jnp.float32)
    site = data_ref[:, :here, :].reshape(peers * here, breadth)
    row_ids = lax.broadcasted_iota(jnp.int32, site.shape, 0)
    alive = jnp.logical_and(row_ids < meta[0], column_ids < live_pair)
    site = jnp.where(alive, site, 0.0)
    full_scale = math.sqrt(4 * peers * here)
    one = dot(site[:, :HALF], kept[:, :HALF], 1, 1)
    two = site[:, HALF:] - dot(one, kept[:, HALF : 2 * HALF], 1, 0)
    two = dot(two, first[:, HALF:], 1, 1)
    out_ref[:, :here, :HALF] = (full_scale * one).reshape(peers, here, HALF)
    out_ref[:, :here, HALF:] = (full_scale * two).reshape(peers, here, HALF)

    squares = jnp.sum(gram_ref[slot_rows(6), :], axis=0, keepdims=True)
    scale = lax.rsqrt(squares * (1.0 / entries) + 1e-06)
    nxt = data_ref[:, here:, :].reshape(peers * STEP, breadth)
    nxt = jnp.where(column_ids < live_slot, nxt, 0.0)
    one = dot(nxt[:, :HALF], kept[:, 2 * HALF : 3 * HALF], 1, 1) + dot(
        nxt[:, HALF:], kept[:, 3 * HALF :], 1, 1
    )
    two = dot(nxt[:, HALF:], second[:, :HALF], 1, 1)
    out_ref[:, here:, :HALF] = (scale * one).reshape(peers, STEP, HALF)
    out_ref[:, here:, HALF:] = (scale * two).reshape(peers, STEP, HALF)


def body(site_blocks, row_lengths, column_lengths, joining, owner_slots, next_blocks):
    sector_count, states, row_count, breadth = site_blocks.shape
    slots, local_columns = next_blocks.shape[:2]
    n_row = lax.axis_size("row")
    n_all = n_row * lax.axis_size("grp")
    both = ("grp", "row")
    me = lax.axis_index("grp") * n_row + lax.axis_index("row")
    quarters = n_row // slots
    piece_columns = local_columns // quarters
    sent = pl.pallas_call(
        gather_kernel,
        out_shape=jax.ShapeDtypeStruct((n_row, row_count + piece_columns, breadth), jnp.float32),
        in_specs=[HBM, HBM],
        out_specs=VMEM,
        scratch_shapes=[pltpu.SemaphoreType.DMA((2,))],
        compiler_params=PARAMS,
        name="gather",
    )(
        site_blocks.reshape(n_row, row_count, breadth),
        next_blocks.reshape(n_row, piece_columns, breadth),
    )
    join_flat = joining.reshape(-1)
    owner_flat = jnp.repeat(owner_slots, quarters)
    rows_flat = jnp.repeat(row_lengths, states)
    meta = jnp.stack([rows_flat[me], join_flat[me], owner_flat[me]])
    join_row = join_flat.reshape(1, n_all)
    join_col = join_flat.reshape(n_all, 1)
    owner_col = owner_flat.reshape(n_all, 1)
    rows_row = rows_flat.reshape(1, n_all).astype(jnp.float32)

    def swap(x):
        slots_of = x.reshape(n_all, SLOT, HALF)
        return lax.all_to_all(slots_of, both, 0, 0, tiled=True).reshape(x.shape)

    data = lax.all_to_all(sent, "row", 0, 0, tiled=True)
    gram = pl.pallas_call(
        gram_kernel,
        out_shape=jax.ShapeDtypeStruct((n_all * SLOT, HALF), jnp.float32),
        in_specs=[SMEM, SMEM, VMEM, VMEM, VMEM, VMEM, VMEM],
        out_specs=VMEM,
        compiler_params=PARAMS,
        name="gram",
    )(meta, column_lengths, join_row, rows_row, join_col, owner_col, data)
    pieces = swap(gram)
    rows = pl.pallas_call(
        combine_kernel,
        out_shape=jax.ShapeDtypeStruct((n_all * SLOT, HALF), jnp.float32),
        in_specs=[VMEM, VMEM, VMEM, VMEM],
        out_specs=VMEM,
        compiler_params=PARAMS,
        name="combine",
    )(join_row, join_col, owner_col, pieces)
    grams = swap(rows)
    entries = float(n_row * local_columns * breadth * slots * lax.axis_size("grp"))
    result = pl.pallas_call(
        functools.partial(apply_kernel, entries),
        out_shape=jax.ShapeDtypeStruct(sent.shape, jnp.float32),
        in_specs=[SMEM, SMEM, VMEM, VMEM, VMEM, VMEM],
        out_specs=VMEM,
        scratch_shapes=[
            pltpu.VMEM((HALF, 2 * HALF), jnp.float32),
            pltpu.VMEM((HALF, 2 * HALF), jnp.float32),
            pltpu.VMEM((HALF, 4 * HALF), jnp.float32),
        ],
        compiler_params=PARAMS,
        name="factor_apply",
    )(meta, column_lengths, join_row, rows_row, data, grams)
    back = lax.all_to_all(result, "row", 0, 0, tiled=True)
    canonical, next_site = pl.pallas_call(
        scatter_kernel,
        out_shape=(
            jax.ShapeDtypeStruct((n_row, row_count, breadth), jnp.float32),
            jax.ShapeDtypeStruct((n_row, piece_columns, breadth), jnp.float32),
        ),
        in_specs=[VMEM],
        out_specs=(HBM, HBM),
        scratch_shapes=[pltpu.SemaphoreType.DMA((2,))],
        compiler_params=PARAMS,
        name="scatter",
    )(back)
    canonical = canonical.reshape(site_blocks.shape)
    next_site = next_site.reshape(next_blocks.shape)
    return (canonical, next_site)


def solution(mesh):
    in_specs = (P("grp", None, "row", None), P(), P(), P(), P(), P("grp", "row", None))
    out_specs = (P("grp", None, "row", None), P("grp", "row", None))
    return jax.shard_map(body, mesh=mesh, in_specs=in_specs, out_specs=out_specs, check_vma=False)
```

```python
import functools
import math

import jax
import jax.numpy as jnp
from jax import lax
from jax.experimental import pallas as pl
from jax.experimental.pallas import tpu as pltpu
from jax.sharding import PartitionSpec as P

PRECISE = lax.Precision.HIGHEST
HALF = 128
STEP = 8
SLOT = 5
HBM = pl.BlockSpec(memory_space=pltpu.HBM)
PARAMS = pltpu.CompilerParams(vmem_limit_bytes=16 * 1024 * 1024)
VMEM = pl.BlockSpec(memory_space=pltpu.VMEM)
SMEM = pl.BlockSpec(memory_space=pltpu.SMEM)


def dot(a, b, ca, cb):
    return lax.dot_general(
        a, b, (((ca,), (cb,)), ((), ())), precision=PRECISE, preferred_element_type=jnp.float32
    )


def live_count(join_row, rows_row, column_lengths, sector):
    joined = jnp.where(join_row[...] == sector, rows_row[...], 0.0)
    joined = jnp.sum(joined, axis=1, keepdims=True)
    return jnp.minimum(jnp.floor(joined * 0.5), column_lengths[sector].astype(jnp.float32))


def gather_kernel(site_ref, next_ref, out_ref, sems):
    here = site_ref.shape[1]
    one = pltpu.make_async_copy(site_ref, out_ref.at[:, :here, :], sems.at[0])
    two = pltpu.make_async_copy(next_ref, out_ref.at[:, here:, :], sems.at[1])
    one.start()
    two.start()
    one.wait()
    two.wait()


def scatter_kernel(data_ref, site_ref, next_ref, sems):
    here = site_ref.shape[1]
    one = pltpu.make_async_copy(data_ref.at[:, :here, :], site_ref, sems.at[0])
    two = pltpu.make_async_copy(data_ref.at[:, here:, :], next_ref, sems.at[1])
    one.start()
    two.start()
    one.wait()
    two.wait()


def slot_rows(index):
    return pl.ds(index, HALF, stride=SLOT)


def gram_kernel(meta, column_lengths, join_row, rows_row, unused_one, unused_two, data_ref, out_ref):
    peers, depth, breadth = data_ref.shape
    here = depth - STEP
    site = data_ref[:, :here, :].reshape(peers * here, breadth)
    row_ids = lax.broadcasted_iota(jnp.int32, site.shape, 0)
    site = jnp.where(row_ids < meta[0], site, 0.0)
    nxt = data_ref[:, here:, :].reshape(peers * STEP, breadth)
    live_slot = live_count(join_row, rows_row, column_lengths, meta[2])
    column_ids = lax.broadcasted_iota(jnp.int32, (1, breadth), 1).astype(jnp.float32)
    nxt = jnp.where(column_ids < live_slot, nxt, 0.0)
    sub = lax.broadcasted_iota(jnp.int32, (HALF, HALF), 0)
    lane = lax.broadcasted_iota(jnp.int32, (HALF, HALF), 1)
    diagonals = []
    for start, block in ((0, site), (2, nxt)):
        top = dot(block[:, :HALF], block, 0, 0)
        low = dot(block[:, HALF:], block[:, HALF:], 0, 0)
        out_ref[slot_rows(start), :] = jnp.where(sub <= lane, top[:, :HALF], low)
        out_ref[slot_rows(start + 1), :] = top[:, HALF:]
        diagonals.append(jnp.sum(jnp.where(sub == lane, low, 0.0), axis=1, keepdims=True))
    out_ref[slot_rows(4), :] = jnp.where(lane < HALF // 2, diagonals[0], diagonals[1])


def combine_kernel(meta, join_row, join_col, owner_col, piece_ref, out_ref):
    packed, cross, diagonal = (slice(i * HALF, (i + 1) * HALF) for i in range(3))
    piece = jnp.concatenate([piece_ref[slot_rows(i), :] for i in (0, 1, 4)], axis=1)
    pair_hot = (join_col[...] == join_row[...]).astype(jnp.float32)
    slot_hot = (owner_col[...] == join_row[...]).astype(jnp.float32)
    pair_part = dot(pair_hot, piece, 1, 0)
    slot_part = dot(slot_hot, piece, 1, 0)
    out_ref[slot_rows(0), :] = pair_part[:, packed]
    out_ref[slot_rows(1), :] = pair_part[:, cross]
    out_ref[slot_rows(2), :] = slot_part[:, packed]
    out_ref[slot_rows(3), :] = slot_part[:, cross]
    lane = lax.broadcasted_iota(jnp.int32, (1, HALF), 1)
    norm = jnp.where(lane == meta[3], 1.0, 2.0) * slot_part[:, packed] * piece_ref[slot_rows(2), :]
    norm = norm + 2.0 * slot_part[:, cross] * piece_ref[slot_rows(3), :]
    moment = jnp.where(lane == HALF - 1, pltpu.roll(slot_part[:, diagonal], HALF // 2, 1), 0.0)
    norm = norm + moment * piece_ref[slot_rows(4), :]
    norm = jnp.sum(jnp.sum(norm, axis=0, keepdims=True), axis=1, keepdims=True)
    quarter = HALF // 4
    pair_diagonal = jnp.broadcast_to(pair_part[:, 2 * HALF : 2 * HALF + 1], (HALF, HALF))
    slot_diagonal = jnp.broadcast_to(slot_part[:, 2 * HALF : 2 * HALF + 1], (HALF, HALF))
    last = jnp.where(lane < quarter, pair_diagonal, slot_diagonal)
    out_ref[slot_rows(4), :] = jnp.where(lane < 2 * quarter, last, norm)


def split(x):
    high = x.astype(jnp.bfloat16).astype(jnp.float32)
    rest = x - high
    middle = rest.astype(jnp.bfloat16).astype(jnp.float32)
    return high, middle, rest - middle


def eliminate(first, second):
    shape = (STEP, HALF)
    sub = lax.broadcasted_iota(jnp.int32, shape, 0)
    lane = lax.broadcasted_iota(jnp.int32, shape, 1)
    upper_half = sub < STEP // 2

    def load(row, side):
        cut = slice(side * HALF, (side + 1) * HALF)
        one = jnp.broadcast_to(first[row : row + 1, cut], shape)
        two = jnp.broadcast_to(second[row : row + 1, cut], shape)
        return jnp.where(upper_half, one, two)

    def spread(x, column):
        return jnp.broadcast_to(x[:, column : column + 1], shape)

    sides = [[load(i, side) for i in range(STEP)] for side in (0, 1)]
    for start in range(0, HALF, STEP):
        after = start + STEP
        a = [[spread(sides[0][i], start + j) for i in range(j + 1)] for j in range(STEP)]
        following = None
        if after < HALF:
            following = [[load(after + i, side) for i in range(STEP)] for side in (0, 1)]
        for k in range(STEP):
            root = lax.rsqrt(a[k][k])
            for j in range(k + 1, STEP):
                a[j][k] = a[j][k] * root
            for j in range(k + 1, STEP):
                for i in range(k + 1, j + 1):
                    a[j][i] = a[j][i] - a[j][k] * a[i][k]
            for rows in sides:
                rows[k] = rows[k] * root
                for j in range(k + 1, STEP):
                    rows[j] = rows[j] - a[j][k] * rows[k]
            if following is not None:
                for i in range(STEP):
                    factor = spread(sides[0][k], after + i)
                    for rows, later in zip(sides, following):
                        later[i] = later[i] - factor * rows[k]

        panels = [[], []]
        for rows in sides:
            straight, crossed = rows[0], rows[STEP // 2]
            for k in range(1, STEP):
                straight = jnp.where(sub == k, rows[k], straight)
                crossed = jnp.where(sub == k, rows[(k + STEP // 2) % STEP], crossed)
            crossed = pltpu.roll(crossed, STEP // 2, 0)
            panels[0].append(jnp.where(upper_half, straight, crossed))
            panels[1].append(jnp.where(upper_half, crossed, straight))
        for work_ref, (one, two) in zip((first, second), panels):
            one = jnp.where(lane >= sub + start, one, 0.0)
            panel = jnp.concatenate([one, two], axis=1)
            work_ref[start:after, :] = panel
            if after + STEP < HALF:
                high, middle, low = split(panel)
                lhs = jnp.concatenate([high, high, middle, middle, high, low], axis=0)[:, :HALF]
                rhs = jnp.concatenate([high, middle, high, middle, low, high], axis=0)
                update = lax.dot_general(
                    lhs.astype(jnp.bfloat16),
                    rhs.astype(jnp.bfloat16),
                    (((0,), (0,)), ((), ())),
                    preferred_element_type=jnp.float32,
                )
                rest = slice(after + STEP, HALF)
                work_ref[rest, :] = work_ref[rest, :] - update[rest, :]
        sides = following


def apply_kernel(
    entries, meta, column_lengths, join_row, rows_row, data_ref, gram_ref, out_ref, first, second, kept
):
    peers, depth, breadth = data_ref.shape
    here = depth - STEP
    live_pair = live_count(join_row, rows_row, column_lengths, meta[1])
    live_slot = live_count(join_row, rows_row, column_lengths, meta[2])
    sub = lax.broadcasted_iota(jnp.int32, (HALF, HALF), 0)
    lane = lax.broadcasted_iota(jnp.int32, (HALF, HALF), 1)
    eye = jnp.where(sub == lane, 1.0, 0.0)
    sub = sub.astype(jnp.float32)
    lane = lane.astype(jnp.float32)

    lasts = gram_ref[slot_rows(4), :]

    def masked(start, live, row_from, col_from):
        block = gram_ref[slot_rows(start), :]
        if row_from:
            column = start * HALF // 8
            block = jnp.where(sub == lane, lasts[:, column : column + 1], block.T)
        alive = jnp.logical_and(sub + row_from < live, lane + col_from < live)
        return jnp.where(alive, block, eye if row_from == col_from else 0.0)

    first[:, :HALF] = masked(0, live_pair, 0, 0)
    first[:, HALF:] = eye
    second[:, :HALF] = masked(2, live_slot, 0, 0)
    second[:, HALF:] = masked(3, live_slot, 0, HALF)

    def half(index, carry):
        eliminate(first, second)

        @pl.when(index == 0)
        def _():
            pair_turn = first[:, HALF:]
            pair_cross = dot(pair_turn, masked(1, live_pair, 0, HALF), 1, 0)
            slot_cross = second[:, HALF:]
            kept[:, :HALF] = pair_turn
            kept[:, HALF : 2 * HALF] = pair_cross
            kept[:, 2 * HALF : 4 * HALF] = second[...]
            first[:, :HALF] = masked(0, live_pair, HALF, HALF) - dot(
                pair_cross, pair_cross, 0, 0
            )
            first[:, HALF:] = eye
            second[:, :HALF] = masked(2, live_slot, HALF, HALF) - dot(
                slot_cross, slot_cross, 0, 0
            )

        return carry

    lax.fori_loop(0, 2, half, 0)

    column_ids = lax.broadcasted_iota(jnp.int32, (1, breadth), 1).astype(jnp.float32)
    site = data_ref[:, :here, :].reshape(peers * here, breadth)
    row_ids = lax.broadcasted_iota(jnp.int32, site.shape, 0)
    alive = jnp.logical_and(row_ids < meta[0], column_ids < live_pair)
    site = jnp.where(alive, site, 0.0)
    full_scale = math.sqrt(4 * peers * here)
    one = dot(site[:, :HALF], kept[:, :HALF], 1, 1)
    two = site[:, HALF:] - dot(one, kept[:, HALF : 2 * HALF], 1, 0)
    two = dot(two, first[:, HALF:], 1, 1)
    out_ref[:, :here, :HALF] = (full_scale * one).reshape(peers, here, HALF)
    out_ref[:, :here, HALF:] = (full_scale * two).reshape(peers, here, HALF)

    squares = jnp.sum(lasts, axis=0, keepdims=True)[:, HALF - 1 :]
    scale = lax.rsqrt(squares * (1.0 / entries) + 1e-06)
    nxt = data_ref[:, here:, :].reshape(peers * STEP, breadth)
    nxt = jnp.where(column_ids < live_slot, nxt, 0.0)
    one = dot(nxt[:, :HALF], kept[:, 2 * HALF : 3 * HALF], 1, 1) + dot(
        nxt[:, HALF:], kept[:, 3 * HALF :], 1, 1
    )
    two = dot(nxt[:, HALF:], second[:, :HALF], 1, 1)
    out_ref[:, here:, :HALF] = (scale * one).reshape(peers, STEP, HALF)
    out_ref[:, here:, HALF:] = (scale * two).reshape(peers, STEP, HALF)


def body(site_blocks, row_lengths, column_lengths, joining, owner_slots, next_blocks):
    sector_count, states, row_count, breadth = site_blocks.shape
    slots, local_columns = next_blocks.shape[:2]
    n_row = lax.axis_size("row")
    n_all = n_row * lax.axis_size("grp")
    both = ("grp", "row")
    me = lax.axis_index("grp") * n_row + lax.axis_index("row")
    quarters = n_row // slots
    piece_columns = local_columns // quarters
    sent = pl.pallas_call(
        gather_kernel,
        out_shape=jax.ShapeDtypeStruct((n_row, row_count + piece_columns, breadth), jnp.float32),
        in_specs=[HBM, HBM],
        out_specs=VMEM,
        scratch_shapes=[pltpu.SemaphoreType.DMA((2,))],
        compiler_params=PARAMS,
        name="gather",
    )(
        site_blocks.reshape(n_row, row_count, breadth),
        next_blocks.reshape(n_row, piece_columns, breadth),
    )
    join_flat = joining.reshape(-1)
    owner_flat = jnp.repeat(owner_slots, quarters)
    rows_flat = jnp.repeat(row_lengths, states)
    meta = jnp.stack([rows_flat[me], join_flat[me], owner_flat[me], me])
    join_row = join_flat.reshape(1, n_all)
    join_col = join_flat.reshape(n_all, 1)
    owner_col = owner_flat.reshape(n_all, 1)
    rows_row = rows_flat.reshape(1, n_all).astype(jnp.float32)

    def swap(x):
        slots_of = x.reshape(n_all, 1, SLOT * HALF)
        return lax.all_to_all(slots_of, both, 0, 0, tiled=True).reshape(x.shape)

    data = lax.all_to_all(sent, "row", 0, 0, tiled=True)
    gram = pl.pallas_call(
        gram_kernel,
        out_shape=jax.ShapeDtypeStruct((n_all * SLOT, HALF), jnp.float32),
        in_specs=[SMEM, SMEM, VMEM, VMEM, VMEM, VMEM, VMEM],
        out_specs=VMEM,
        compiler_params=PARAMS,
        name="gram",
    )(meta, column_lengths, join_row, rows_row, join_col, owner_col, data)
    pieces = swap(gram)
    rows = pl.pallas_call(
        combine_kernel,
        out_shape=jax.ShapeDtypeStruct((n_all * SLOT, HALF), jnp.float32),
        in_specs=[SMEM, VMEM, VMEM, VMEM, VMEM],
        out_specs=VMEM,
        compiler_params=PARAMS,
        name="combine",
    )(meta, join_row, join_col, owner_col, pieces)
    grams = swap(rows)
    entries = float(n_row * local_columns * breadth * slots * lax.axis_size("grp"))
    result = pl.pallas_call(
        functools.partial(apply_kernel, entries),
        out_shape=jax.ShapeDtypeStruct(sent.shape, jnp.float32),
        in_specs=[SMEM, SMEM, VMEM, VMEM, VMEM, VMEM],
        out_specs=VMEM,
        scratch_shapes=[
            pltpu.VMEM((HALF, 2 * HALF), jnp.float32),
            pltpu.VMEM((HALF, 2 * HALF), jnp.float32),
            pltpu.VMEM((HALF, 4 * HALF), jnp.float32),
        ],
        compiler_params=PARAMS,
        name="factor_apply",
    )(meta, column_lengths, join_row, rows_row, data, grams)
    back = lax.all_to_all(result, "row", 0, 0, tiled=True)
    canonical, next_site = pl.pallas_call(
        scatter_kernel,
        out_shape=(
            jax.ShapeDtypeStruct((n_row, row_count, breadth), jnp.float32),
            jax.ShapeDtypeStruct((n_row, piece_columns, breadth), jnp.float32),
        ),
        in_specs=[VMEM],
        out_specs=(HBM, HBM),
        scratch_shapes=[pltpu.SemaphoreType.DMA((2,))],
        compiler_params=PARAMS,
        name="scatter",
    )(back)
    canonical = canonical.reshape(site_blocks.shape)
    next_site = next_site.reshape(next_blocks.shape)
    return (canonical, next_site)


def solution(mesh):
    in_specs = (P("grp", None, "row", None), P(), P(), P(), P(), P("grp", "row", None))
    out_specs = (P("grp", None, "row", None), P("grp", "row", None))
    return jax.shard_map(body, mesh=mesh, in_specs=in_specs, out_specs=out_specs, check_vma=False)
```

```python
import functools
import math

import jax
import jax.numpy as jnp
from jax import lax
from jax.experimental import pallas as pl
from jax.experimental.pallas import tpu as pltpu
from jax.sharding import PartitionSpec as P

PRECISE = lax.Precision.HIGHEST
HALF = 128
STEP = 8
SLOT = 5
WHEN = 4
SHARES = 4
HBM = pl.BlockSpec(memory_space=pltpu.HBM)
PARAMS = pltpu.CompilerParams(vmem_limit_bytes=16 * 1024 * 1024)
VMEM = pl.BlockSpec(memory_space=pltpu.VMEM)
SMEM = pl.BlockSpec(memory_space=pltpu.SMEM)


def dot(a, b, ca, cb):
    return lax.dot_general(
        a, b, (((ca,), (cb,)), ((), ())), precision=PRECISE, preferred_element_type=jnp.float32
    )


def live_count(join_row, rows_row, column_lengths, sector):
    joined = jnp.where(join_row[...] == sector, rows_row[...], 0.0)
    joined = jnp.sum(joined, axis=1, keepdims=True)
    return jnp.minimum(jnp.floor(joined * 0.5), column_lengths[sector].astype(jnp.float32))


def gather_kernel(site_ref, next_ref, out_ref, held, in_sems, out_sems):
    here = site_ref.shape[1]
    share = site_ref.shape[0] // SHARES
    cuts = [pl.ds(i * share, share) for i in range(SHARES)]
    arrivals = [
        (
            pltpu.make_async_copy(site_ref.at[cut], held.at[cut, :here, :], in_sems.at[i, 0]),
            pltpu.make_async_copy(next_ref.at[cut], held.at[cut, here:, :], in_sems.at[i, 1]),
        )
        for i, cut in enumerate(cuts)
    ]
    leaves = [pltpu.make_async_copy(held.at[cut], out_ref.at[cut], out_sems.at[i]) for i, cut in enumerate(cuts)]
    for pair in arrivals:
        pair[0].start()
        pair[1].start()
    for pair, leave in zip(arrivals, leaves):
        pair[0].wait()
        pair[1].wait()
        leave.start()
    for leave in leaves:
        leave.wait()


def scatter_kernel(data_ref, site_ref, next_ref, sems):
    here = site_ref.shape[1]
    one = pltpu.make_async_copy(data_ref.at[:, :here, :], site_ref, sems.at[0])
    two = pltpu.make_async_copy(data_ref.at[:, here:, :], next_ref, sems.at[1])
    one.start()
    two.start()
    one.wait()
    two.wait()


def slot_rows(index):
    return pl.ds(index, HALF, stride=SLOT)


def gram_kernel(meta, column_lengths, join_row, rows_row, unused_one, unused_two, data_ref, out_ref):
    peers, depth, breadth = data_ref.shape
    here = depth - STEP
    site = data_ref[:, :here, :].reshape(peers * here, breadth)
    row_ids = lax.broadcasted_iota(jnp.int32, site.shape, 0)
    site = jnp.where(row_ids < meta[0], site, 0.0)
    nxt = data_ref[:, here:, :].reshape(peers * STEP, breadth)
    live_slot = live_count(join_row, rows_row, column_lengths, meta[2])
    column_ids = lax.broadcasted_iota(jnp.int32, (1, breadth), 1).astype(jnp.float32)
    nxt = jnp.where(column_ids < live_slot, nxt, 0.0)
    sub = lax.broadcasted_iota(jnp.int32, (HALF, HALF), 0)
    lane = lax.broadcasted_iota(jnp.int32, (HALF, HALF), 1)
    diagonals = []
    for start, block in ((0, site), (2, nxt)):
        top = dot(block[:, :HALF], block, 0, 0)
        low = dot(block[:, HALF:], block[:, HALF:], 0, 0)
        out_ref[slot_rows(start), :] = jnp.where(sub <= lane, top[:, :HALF], low)
        out_ref[slot_rows(start + 1), :] = top[:, HALF:]
        diagonals.append(jnp.sum(jnp.where(sub == lane, low, 0.0), axis=1, keepdims=True))
    out_ref[slot_rows(4), :] = jnp.where(lane < HALF // 2, diagonals[0], diagonals[1])


def split(x):
    high = x.astype(jnp.bfloat16).astype(jnp.float32)
    rest = x - high
    middle = rest.astype(jnp.bfloat16).astype(jnp.float32)
    return high, middle, rest - middle


def combine_kernel(meta, join_row, join_col, owner_col, piece_ref, out_ref):
    packed, cross, diagonal = (slice(i * HALF, (i + 1) * HALF) for i in range(3))
    piece = jnp.concatenate([piece_ref[slot_rows(i), :] for i in (0, 1, 4)], axis=1)
    hot = jnp.concatenate([join_col[...] == join_row[...], owner_col[...] == join_row[...]], axis=0)
    hot = hot.astype(jnp.float32).astype(jnp.bfloat16)
    parts = 0.0
    for part in split(piece)[::-1]:
        parts = parts + lax.dot_general(
            hot,
            part.astype(jnp.bfloat16),
            (((1,), (0,)), ((), ())),
            preferred_element_type=jnp.float32,
        )
    pair_part, slot_part = parts[:HALF], parts[HALF:]
    out_ref[slot_rows(0), :] = pair_part[:, packed]
    out_ref[slot_rows(1), :] = pair_part[:, cross]
    out_ref[slot_rows(2), :] = slot_part[:, packed]
    out_ref[slot_rows(3), :] = slot_part[:, cross]
    lane = lax.broadcasted_iota(jnp.int32, (1, HALF), 1)
    norm = jnp.where(lane == meta[3], 1.0, 2.0) * slot_part[:, packed] * piece_ref[slot_rows(2), :]
    norm = norm + 2.0 * slot_part[:, cross] * piece_ref[slot_rows(3), :]
    moment = jnp.where(lane == HALF - 1, pltpu.roll(slot_part[:, diagonal], HALF // 2, 1), 0.0)
    norm = norm + moment * piece_ref[slot_rows(4), :]
    norm = jnp.sum(jnp.sum(norm, axis=0, keepdims=True), axis=1, keepdims=True)
    quarter = HALF // 4
    pair_diagonal = jnp.broadcast_to(pair_part[:, 2 * HALF : 2 * HALF + 1], (HALF, HALF))
    slot_diagonal = jnp.broadcast_to(slot_part[:, 2 * HALF : 2 * HALF + 1], (HALF, HALF))
    last = jnp.where(lane < quarter, pair_diagonal, slot_diagonal)
    out_ref[slot_rows(4), :] = jnp.where(lane < 2 * quarter, last, norm)


def product(x, w, contract):
    parts = [p.astype(jnp.bfloat16) for p in split(x)]
    high, middle, low = (p.astype(jnp.bfloat16) for p in split(w))
    wide = jnp.concatenate([parts[0], parts[1]], axis=1)
    tall = jnp.concatenate([parts[0], parts[2]], axis=1)
    inner, outer = contract, 1 - contract
    one = jnp.concatenate(
        [jnp.concatenate([p, p], axis=inner) for p in (high, middle)], axis=outer
    )
    two = jnp.concatenate([low, high], axis=inner)
    dims = (((1,), (inner,)), ((), ()))
    main = lax.dot_general(wide, one, dims, preferred_element_type=jnp.float32)
    rest = lax.dot_general(tall, two, dims, preferred_element_type=jnp.float32)
    width = w.shape[outer]
    return main[:, :width] + (main[:, width:] + rest)


def eliminate(first, second, turn):
    shape = (STEP, HALF)
    sub = lax.broadcasted_iota(jnp.int32, shape, 0)
    lane = lax.broadcasted_iota(jnp.int32, shape, 1)
    upper_half = sub < STEP // 2

    def load(row, side):
        cut = slice(side * HALF, (side + 1) * HALF)
        one = jnp.broadcast_to(first[row : row + 1, cut], shape)
        two = jnp.broadcast_to(second[row : row + 1, cut], shape)
        return jnp.where(upper_half, one, two)

    def spread(x, column):
        return jnp.broadcast_to(x[:, column : column + 1], shape)

    def finish(start, sides):
        after = start + STEP
        panels = [[], []]
        for rows in sides:
            straight, crossed = rows[0], rows[STEP // 2]
            for k in range(1, STEP):
                straight = jnp.where(sub == k, rows[k], straight)
                crossed = jnp.where(sub == k, rows[(k + STEP // 2) % STEP], crossed)
            crossed = pltpu.roll(crossed, STEP // 2, 0)
            panels[0].append(jnp.where(upper_half, straight, crossed))
            panels[1].append(jnp.where(upper_half, crossed, straight))
        for work_ref, (one, two) in zip((first, second), panels):
            one = jnp.where(lane >= sub + start, one, 0.0)
            panel = jnp.concatenate([one, two], axis=1)
            work_ref[start:after, :] = panel
            if after + STEP < HALF:
                high, middle, low = split(panel)
                lhs = jnp.concatenate([high, high, middle, middle, high, low], axis=0)[:, :HALF]
                rhs = jnp.concatenate([high, middle, high, middle, low, high], axis=0)
                base = (after + STEP) // 16 * 16
                update = lax.dot_general(
                    lhs.astype(jnp.bfloat16).T[base:],
                    rhs.astype(jnp.bfloat16),
                    (((1,), (0,)), ((), ())),
                    preferred_element_type=jnp.float32,
                )
                rest = slice(after + STEP, HALF)
                work_ref[rest, :] = work_ref[rest, :] - update[after + STEP - base :, :]

    quad = STEP // 2
    sides = [[load(i, side) for i in range(STEP)] for side in (0, 1)]
    done = None
    for start in range(0, HALF, STEP):
        after = start + STEP
        a = [[spread(sides[0][i], start + j) for i in range(j + 1)] for j in range(STEP)]
        following = None
        for k in range(STEP):
            root = lax.rsqrt(a[k][k])
            for j in range(k + 1, STEP):
                a[j][k] = a[j][k] * root
            for j in range(k + 1, STEP):
                for i in range(k + 1, j + 1):
                    a[j][i] = a[j][i] - a[j][k] * a[i][k]
            for rows in sides:
                rows[k] = rows[k] * root
                for j in range(k + 1, STEP):
                    rows[j] = rows[j] - a[j][k] * rows[k]
            if k == WHEN and done is not None:
                finish(*done)
            if after < HALF:
                if following is None:
                    totals = [[None, None], [None, None]]
                    following = True
                for part in (0, 1):
                    index = after + part * quad + sub % quad
                    factor = jnp.take_along_axis(sides[0][k], index, axis=1)
                    for rows, total in zip(sides, totals):
                        term = factor * rows[k]
                        total[part] = term if k == 0 else total[part] + term
        done = (start, sides)
        if after < HALF:
            for side in (0, 1):
                cut = slice(side * HALF, (side + 1) * HALF)
                one, two = first[after : after + STEP, cut], second[after : after + STEP, cut]
                early = jnp.where(upper_half, one, pltpu.roll(two, quad, 0))
                late = jnp.where(upper_half, pltpu.roll(one, quad, 0), two)
                turn[:STEP, cut] = early - totals[side][0]
                turn[STEP:, cut] = late - totals[side][1]

            def reload(i, side):
                cut = slice(side * HALF, (side + 1) * HALF)
                row = i // quad * STEP + i % quad
                one = jnp.broadcast_to(turn[row : row + 1, cut], shape)
                two = jnp.broadcast_to(turn[row + quad : row + quad + 1, cut], shape)
                return jnp.where(upper_half, one, two)

            sides = [[reload(i, side) for i in range(STEP)] for side in (0, 1)]
    finish(*done)


def apply_kernel(
    entries, meta, column_lengths, join_row, rows_row, data_ref, gram_ref, out_ref, first, second, kept, turn
):
    peers, depth, breadth = data_ref.shape
    here = depth - STEP
    live_pair = live_count(join_row, rows_row, column_lengths, meta[1])
    live_slot = live_count(join_row, rows_row, column_lengths, meta[2])
    sub = lax.broadcasted_iota(jnp.int32, (HALF, HALF), 0)
    lane = lax.broadcasted_iota(jnp.int32, (HALF, HALF), 1)
    eye = jnp.where(sub == lane, 1.0, 0.0)
    sub = sub.astype(jnp.float32)
    lane = lane.astype(jnp.float32)

    lasts = gram_ref[slot_rows(4), :]

    def masked(start, live, row_from, col_from):
        block = gram_ref[slot_rows(start), :]
        if row_from:
            column = start * HALF // 8
            block = jnp.where(sub == lane, lasts[:, column : column + 1], block.T)
        alive = jnp.logical_and(sub + row_from < live, lane + col_from < live)
        return jnp.where(alive, block, eye if row_from == col_from else 0.0)

    first[:, :HALF] = masked(0, live_pair, 0, 0)
    first[:, HALF:] = eye
    second[:, :HALF] = masked(2, live_slot, 0, 0)
    second[:, HALF:] = masked(3, live_slot, 0, HALF)

    def half(index, carry):
        eliminate(first, second, turn)

        @pl.when(index == 0)
        def _():
            pair_turn = first[:, HALF:]
            pair_cross = dot(pair_turn, masked(1, live_pair, 0, HALF), 1, 0)
            slot_cross = second[:, HALF:]
            kept[:, :HALF] = pair_turn
            kept[:, HALF : 2 * HALF] = pair_cross
            kept[:, 2 * HALF : 4 * HALF] = second[...]
            first[:, :HALF] = masked(0, live_pair, HALF, HALF) - dot(
                pair_cross, pair_cross, 0, 0
            )
            first[:, HALF:] = eye
            second[:, :HALF] = masked(2, live_slot, HALF, HALF) - dot(
                slot_cross, slot_cross, 0, 0
            )

        return carry

    lax.fori_loop(0, 2, half, 0)

    column_ids = lax.broadcasted_iota(jnp.int32, (1, breadth), 1).astype(jnp.float32)
    site = data_ref[:, :here, :].reshape(peers * here, breadth)
    row_ids = lax.broadcasted_iota(jnp.int32, site.shape, 0)
    alive = jnp.logical_and(row_ids < meta[0], column_ids < live_pair)
    site = jnp.where(alive, site, 0.0)
    full_scale = math.sqrt(4 * peers * here)
    one = product(site[:, :HALF], kept[:, :HALF], 1)
    two = site[:, HALF:] - product(one, kept[:, HALF : 2 * HALF], 0)
    two = product(two, first[:, HALF:], 1)
    out_ref[:, :here, :HALF] = (full_scale * one).reshape(peers, here, HALF)
    out_ref[:, :here, HALF:] = (full_scale * two).reshape(peers, here, HALF)

    squares = jnp.sum(lasts, axis=0, keepdims=True)[:, HALF - 1 :]
    scale = lax.rsqrt(squares * (1.0 / entries) + 1e-06)
    nxt = data_ref[:, here:, :].reshape(peers * STEP, breadth)
    nxt = jnp.where(column_ids < live_slot, nxt, 0.0)
    one = product(nxt[:, :HALF], kept[:, 2 * HALF : 3 * HALF], 1) + product(
        nxt[:, HALF:], kept[:, 3 * HALF :], 1
    )
    two = product(nxt[:, HALF:], second[:, :HALF], 1)
    out_ref[:, here:, :HALF] = (scale * one).reshape(peers, STEP, HALF)
    out_ref[:, here:, HALF:] = (scale * two).reshape(peers, STEP, HALF)


def body(site_blocks, row_lengths, column_lengths, joining, owner_slots, next_blocks):
    sector_count, states, row_count, breadth = site_blocks.shape
    slots, local_columns = next_blocks.shape[:2]
    n_row = lax.axis_size("row")
    n_all = n_row * lax.axis_size("grp")
    both = ("grp", "row")
    me = lax.axis_index("grp") * n_row + lax.axis_index("row")
    quarters = n_row // slots
    piece_columns = local_columns // quarters
    sent = pl.pallas_call(
        gather_kernel,
        out_shape=jax.ShapeDtypeStruct((n_row, row_count + piece_columns, breadth), jnp.float32),
        in_specs=[HBM, HBM],
        out_specs=HBM,
        scratch_shapes=[
            pltpu.VMEM((n_row, row_count + piece_columns, breadth), jnp.float32),
            pltpu.SemaphoreType.DMA((SHARES, 2)),
            pltpu.SemaphoreType.DMA((SHARES,)),
        ],
        compiler_params=pltpu.CompilerParams(vmem_limit_bytes=60 * 1024 * 1024),
        name="gather",
    )(
        site_blocks.reshape(n_row, row_count, breadth),
        next_blocks.reshape(n_row, piece_columns, breadth),
    )
    join_flat = joining.reshape(-1)
    owner_flat = jnp.repeat(owner_slots, quarters)
    rows_flat = jnp.repeat(row_lengths, states)
    meta = jnp.stack([rows_flat[me], join_flat[me], owner_flat[me], me])
    join_row = join_flat.reshape(1, n_all)
    join_col = join_flat.reshape(n_all, 1)
    owner_col = owner_flat.reshape(n_all, 1)
    rows_row = rows_flat.reshape(1, n_all).astype(jnp.float32)

    def swap(x):
        slots_of = x.reshape(n_all, 1, SLOT * HALF)
        return lax.all_to_all(slots_of, both, 0, 0, tiled=True).reshape(x.shape)

    data = lax.all_to_all(sent, "row", 0, 0, tiled=True)
    gram = pl.pallas_call(
        gram_kernel,
        out_shape=jax.ShapeDtypeStruct((n_all * SLOT, HALF), jnp.float32),
        in_specs=[SMEM, SMEM, VMEM, VMEM, VMEM, VMEM, VMEM],
        out_specs=VMEM,
        compiler_params=PARAMS,
        name="gram",
    )(meta, column_lengths, join_row, rows_row, join_col, owner_col, data)
    pieces = swap(gram)
    rows = pl.pallas_call(
        combine_kernel,
        out_shape=jax.ShapeDtypeStruct((n_all * SLOT, HALF), jnp.float32),
        in_specs=[SMEM, VMEM, VMEM, VMEM, VMEM],
        out_specs=VMEM,
        compiler_params=PARAMS,
        name="combine",
    )(meta, join_row, join_col, owner_col, pieces)
    grams = swap(rows)
    entries = float(n_row * local_columns * breadth * slots * lax.axis_size("grp"))
    result = pl.pallas_call(
        functools.partial(apply_kernel, entries),
        out_shape=jax.ShapeDtypeStruct(sent.shape, jnp.float32),
        in_specs=[SMEM, SMEM, VMEM, VMEM, VMEM, VMEM],
        out_specs=VMEM,
        scratch_shapes=[
            pltpu.VMEM((HALF, 2 * HALF), jnp.float32),
            pltpu.VMEM((HALF, 2 * HALF), jnp.float32),
            pltpu.VMEM((HALF, 4 * HALF), jnp.float32),
            pltpu.VMEM((2 * STEP, 2 * HALF), jnp.float32),
        ],
        compiler_params=PARAMS,
        name="factor_apply",
    )(meta, column_lengths, join_row, rows_row, data, grams)
    back = lax.all_to_all(result, "row", 0, 0, tiled=True)
    canonical, next_site = pl.pallas_call(
        scatter_kernel,
        out_shape=(
            jax.ShapeDtypeStruct((n_row, row_count, breadth), jnp.float32),
            jax.ShapeDtypeStruct((n_row, piece_columns, breadth), jnp.float32),
        ),
        in_specs=[VMEM],
        out_specs=(HBM, HBM),
        scratch_shapes=[pltpu.SemaphoreType.DMA((2,))],
        compiler_params=PARAMS,
        name="scatter",
    )(back)
    canonical = canonical.reshape(site_blocks.shape)
    next_site = next_site.reshape(next_blocks.shape)
    return (canonical, next_site)


def solution(mesh):
    in_specs = (P("grp", None, "row", None), P(), P(), P(), P(), P("grp", "row", None))
    out_specs = (P("grp", None, "row", None), P("grp", "row", None))
    return jax.shard_map(body, mesh=mesh, in_specs=in_specs, out_specs=out_specs, check_vma=False)
```

```python
import functools
import math

import jax
import jax.numpy as jnp
from jax import lax
from jax.experimental import pallas as pl
from jax.experimental.pallas import tpu as pltpu
from jax.sharding import PartitionSpec as P

PRECISE = lax.Precision.HIGHEST
HALF = 128
STEP = 8
SLOT = 5
WHEN = 4
HBM = pl.BlockSpec(memory_space=pltpu.HBM)
PARAMS = pltpu.CompilerParams(vmem_limit_bytes=16 * 1024 * 1024)
VMEM = pl.BlockSpec(memory_space=pltpu.VMEM)
SMEM = pl.BlockSpec(memory_space=pltpu.SMEM)


def dot(a, b, ca, cb):
    return lax.dot_general(
        a, b, (((ca,), (cb,)), ((), ())), precision=PRECISE, preferred_element_type=jnp.float32
    )


def gather_kernel(site_ref, next_ref, out_ref, sems):
    here = site_ref.shape[1]
    one = pltpu.make_async_copy(site_ref, out_ref.at[:, :here, :], sems.at[0])
    two = pltpu.make_async_copy(next_ref, out_ref.at[:, here:, :], sems.at[1])
    one.start()
    two.start()
    one.wait()
    two.wait()


def scatter_kernel(data_ref, site_ref, next_ref, sems):
    here = site_ref.shape[1]
    one = pltpu.make_async_copy(data_ref.at[:, :here, :], site_ref, sems.at[0])
    two = pltpu.make_async_copy(data_ref.at[:, here:, :], next_ref, sems.at[1])
    one.start()
    two.start()
    one.wait()
    two.wait()


def slot_rows(index):
    return pl.ds(index, HALF, stride=SLOT)


def split(x):
    high = x.astype(jnp.bfloat16).astype(jnp.float32)
    rest = x - high
    middle = rest.astype(jnp.bfloat16).astype(jnp.float32)
    return high, middle, rest - middle


def gram_kernel(
    row_lengths,
    column_lengths,
    joining,
    owner_slots,
    rows_ref,
    join_ref,
    owner_ref,
    data_ref,
    out_ref,
    meta_ref,
    live_ref,
    join_row,
    join_col,
    owner_col,
):
    states, sectors = join_ref.shape
    n_row = lax.axis_size("row")
    group, place = lax.axis_index("grp"), lax.axis_index("row")
    left = group * (n_row // states) + place // states
    meta_ref[0] = row_lengths[left]
    meta_ref[1] = group * n_row + place
    joins = join_ref[...]
    for index, sector in enumerate((joining[place % states, left], owner_slots[left])):
        joined = jnp.sum(jnp.where(joins == sector, rows_ref[...], 0), axis=0, keepdims=True)
        joined = jnp.sum(joined.astype(jnp.float32), axis=1, keepdims=True)
        live = jnp.minimum(jnp.floor(joined * 0.5), column_lengths[sector].astype(jnp.float32))
        live_ref[index : index + 1, :] = jnp.broadcast_to(live, (1, HALF))
    lefts = lax.broadcasted_iota(jnp.int32, (sectors, HALF), 0)
    devices = lax.broadcasted_iota(jnp.int32, (sectors, HALF), 1)
    expand = (devices // states == lefts).astype(jnp.float32)
    by_state = dot(joins.astype(jnp.float32), expand, 1, 0)
    state = lax.broadcasted_iota(jnp.int32, (states, HALF), 0)
    device = lax.broadcasted_iota(jnp.int32, (states, HALF), 1)
    row = jnp.sum(jnp.where(device % states == state, by_state, 0.0), axis=0, keepdims=True)
    owners = dot(owner_ref[...].astype(jnp.float32), expand, 1, 0)
    join_row[...] = row
    sub = lax.broadcasted_iota(jnp.int32, (HALF, HALF), 0)
    lane = lax.broadcasted_iota(jnp.int32, (HALF, HALF), 1)
    join_col[...] = jnp.sum(jnp.where(sub == lane, row, 0.0), axis=1, keepdims=True)
    owner_col[...] = jnp.sum(jnp.where(sub == lane, owners, 0.0), axis=1, keepdims=True)
    peers, depth, breadth = data_ref.shape
    here = depth - STEP
    site = data_ref[:, :here, :].reshape(peers * here, breadth)
    row_ids = lax.broadcasted_iota(jnp.int32, site.shape, 0)
    site = jnp.where(row_ids < row_lengths[left], site, 0.0)
    nxt = data_ref[:, here:, :].reshape(peers * STEP, breadth)
    live_slot = live
    column_ids = lax.broadcasted_iota(jnp.int32, (1, breadth), 1).astype(jnp.float32)
    nxt = jnp.where(column_ids < live_slot, nxt, 0.0)
    sub = lax.broadcasted_iota(jnp.int32, (HALF, HALF), 0)
    lane = lax.broadcasted_iota(jnp.int32, (HALF, HALF), 1)
    diagonals = []
    for start, block in ((0, site), (2, nxt)):
        high, middle, low = (part.astype(jnp.bfloat16) for part in split(block))
        dims = (((0,), (0,)), ((), ()))
        wide = lax.dot_general(high, middle, dims, preferred_element_type=jnp.float32)
        wide = wide + lax.dot_general(high, low, dims, preferred_element_type=jnp.float32)
        square = lax.dot_general(high, high, dims, preferred_element_type=jnp.float32)
        square = square + lax.dot_general(middle, middle, dims, preferred_element_type=jnp.float32)
        square = square + (wide + wide.T)
        top, low = square[:HALF], square[HALF:, HALF:]
        out_ref[slot_rows(start), :] = jnp.where(sub <= lane, top[:, :HALF], low)
        out_ref[slot_rows(start + 1), :] = top[:, HALF:]
        diagonals.append(jnp.sum(jnp.where(sub == lane, low, 0.0), axis=1, keepdims=True))
    out_ref[slot_rows(4), :] = jnp.where(lane < HALF // 2, diagonals[0], diagonals[1])


def combine_kernel(meta, join_row, join_col, owner_col, piece_ref, out_ref):
    packed, cross, diagonal = (slice(i * HALF, (i + 1) * HALF) for i in range(3))
    piece = jnp.concatenate([piece_ref[slot_rows(i), :] for i in (0, 1, 4)], axis=1)
    hot = jnp.concatenate([join_col[...] == join_row[...], owner_col[...] == join_row[...]], axis=0)
    hot = hot.astype(jnp.float32).astype(jnp.bfloat16)
    parts = 0.0
    for part in split(piece)[::-1]:
        parts = parts + lax.dot_general(
            hot,
            part.astype(jnp.bfloat16),
            (((1,), (0,)), ((), ())),
            preferred_element_type=jnp.float32,
        )
    pair_part, slot_part = parts[:HALF], parts[HALF:]
    out_ref[slot_rows(0), :] = pair_part[:, packed]
    out_ref[slot_rows(1), :] = pair_part[:, cross]
    out_ref[slot_rows(2), :] = slot_part[:, packed]
    out_ref[slot_rows(3), :] = slot_part[:, cross]
    lane = lax.broadcasted_iota(jnp.int32, (1, HALF), 1)
    norm = jnp.where(lane == meta[1], 1.0, 2.0) * slot_part[:, packed] * piece_ref[slot_rows(2), :]
    norm = norm + 2.0 * slot_part[:, cross] * piece_ref[slot_rows(3), :]
    moment = jnp.where(lane == HALF - 1, pltpu.roll(slot_part[:, diagonal], HALF // 2, 1), 0.0)
    norm = norm + moment * piece_ref[slot_rows(4), :]
    norm = jnp.sum(jnp.sum(norm, axis=0, keepdims=True), axis=1, keepdims=True)
    quarter = HALF // 4
    pair_diagonal = jnp.broadcast_to(pair_part[:, 2 * HALF : 2 * HALF + 1], (HALF, HALF))
    slot_diagonal = jnp.broadcast_to(slot_part[:, 2 * HALF : 2 * HALF + 1], (HALF, HALF))
    last = jnp.where(lane < quarter, pair_diagonal, slot_diagonal)
    out_ref[slot_rows(4), :] = jnp.where(lane < 2 * quarter, last, norm)


def product(x, w, contract):
    parts = [p.astype(jnp.bfloat16) for p in split(x)]
    high, middle, low = (p.astype(jnp.bfloat16) for p in split(w))
    wide = jnp.concatenate([parts[0], parts[1]], axis=1)
    tall = jnp.concatenate([parts[0], parts[2]], axis=1)
    inner, outer = contract, 1 - contract
    one = jnp.concatenate(
        [jnp.concatenate([p, p], axis=inner) for p in (high, middle)], axis=outer
    )
    two = jnp.concatenate([low, high], axis=inner)
    dims = (((1,), (inner,)), ((), ()))
    main = lax.dot_general(wide, one, dims, preferred_element_type=jnp.float32)
    rest = lax.dot_general(tall, two, dims, preferred_element_type=jnp.float32)
    width = w.shape[outer]
    return main[:, :width] + (main[:, width:] + rest)


def eliminate(first, second, turn):
    shape = (STEP, HALF)
    sub = lax.broadcasted_iota(jnp.int32, shape, 0)
    lane = lax.broadcasted_iota(jnp.int32, shape, 1)
    upper_half = sub < STEP // 2

    def load(row, side):
        cut = slice(side * HALF, (side + 1) * HALF)
        one = jnp.broadcast_to(first[row : row + 1, cut], shape)
        two = jnp.broadcast_to(second[row : row + 1, cut], shape)
        return jnp.where(upper_half, one, two)

    def spread(x, column):
        return jnp.broadcast_to(x[:, column : column + 1], shape)

    def finish(start, sides):
        after = start + STEP
        panels = [[], []]
        for rows in sides:
            straight, crossed = rows[0], rows[STEP // 2]
            for k in range(1, STEP):
                straight = jnp.where(sub == k, rows[k], straight)
                crossed = jnp.where(sub == k, rows[(k + STEP // 2) % STEP], crossed)
            crossed = pltpu.roll(crossed, STEP // 2, 0)
            panels[0].append(jnp.where(upper_half, straight, crossed))
            panels[1].append(jnp.where(upper_half, crossed, straight))
        for work_ref, (one, two) in zip((first, second), panels):
            one = jnp.where(lane >= sub + start, one, 0.0)
            panel = jnp.concatenate([one, two], axis=1)
            work_ref[start:after, :] = panel
            if after + STEP < HALF:
                high, middle, low = split(panel)
                lhs = jnp.concatenate([high, high, middle, middle, high, low], axis=0)[:, :HALF]
                rhs = jnp.concatenate([high, middle, high, middle, low, high], axis=0)
                base = (after + STEP) // 16 * 16
                update = lax.dot_general(
                    lhs.astype(jnp.bfloat16).T[base:],
                    rhs.astype(jnp.bfloat16),
                    (((1,), (0,)), ((), ())),
                    preferred_element_type=jnp.float32,
                )
                rest = slice(after + STEP, HALF)
                work_ref[rest, :] = work_ref[rest, :] - update[after + STEP - base :, :]

    quad = STEP // 2
    sides = [[load(i, side) for i in range(STEP)] for side in (0, 1)]
    done = None
    for start in range(0, HALF, STEP):
        after = start + STEP
        a = [[spread(sides[0][i], start + j) for i in range(j + 1)] for j in range(STEP)]
        following = None
        for k in range(STEP):
            root = lax.rsqrt(a[k][k])
            for j in range(k + 1, STEP):
                a[j][k] = a[j][k] * root
            for j in range(k + 1, STEP):
                for i in range(k + 1, j + 1):
                    a[j][i] = a[j][i] - a[j][k] * a[i][k]
            for rows in sides:
                rows[k] = rows[k] * root
                for j in range(k + 1, STEP):
                    rows[j] = rows[j] - a[j][k] * rows[k]
            if k == WHEN and done is not None:
                finish(*done)
            if after < HALF:
                if following is None:
                    totals = [[None, None], [None, None]]
                    following = True
                for part in (0, 1):
                    index = after + part * quad + sub % quad
                    factor = jnp.take_along_axis(sides[0][k], index, axis=1)
                    for rows, total in zip(sides, totals):
                        term = factor * rows[k]
                        total[part] = term if k == 0 else total[part] + term
        done = (start, sides)
        if after < HALF:
            for side in (0, 1):
                cut = slice(side * HALF, (side + 1) * HALF)
                one, two = first[after : after + STEP, cut], second[after : after + STEP, cut]
                early = jnp.where(upper_half, one, pltpu.roll(two, quad, 0))
                late = jnp.where(upper_half, pltpu.roll(one, quad, 0), two)
                turn[:STEP, cut] = early - totals[side][0]
                turn[STEP:, cut] = late - totals[side][1]

            def reload(i, side):
                cut = slice(side * HALF, (side + 1) * HALF)
                row = i // quad * STEP + i % quad
                one = jnp.broadcast_to(turn[row : row + 1, cut], shape)
                two = jnp.broadcast_to(turn[row + quad : row + quad + 1, cut], shape)
                return jnp.where(upper_half, one, two)

            sides = [[reload(i, side) for i in range(STEP)] for side in (0, 1)]
    finish(*done)


def apply_kernel(
    entries, meta, live_ref, data_ref, gram_ref, out_ref, first, second, kept, turn
):
    peers, depth, breadth = data_ref.shape
    here = depth - STEP
    live_pair = live_ref[:1, :1]
    live_slot = live_ref[1:2, :1]
    sub = lax.broadcasted_iota(jnp.int32, (HALF, HALF), 0)
    lane = lax.broadcasted_iota(jnp.int32, (HALF, HALF), 1)
    eye = jnp.where(sub == lane, 1.0, 0.0)
    sub = sub.astype(jnp.float32)
    lane = lane.astype(jnp.float32)

    lasts = gram_ref[slot_rows(4), :]

    def masked(start, live, row_from, col_from):
        block = gram_ref[slot_rows(start), :]
        if row_from:
            column = start * HALF // 8
            block = jnp.where(sub == lane, lasts[:, column : column + 1], block.T)
        alive = jnp.logical_and(sub + row_from < live, lane + col_from < live)
        return jnp.where(alive, block, eye if row_from == col_from else 0.0)

    first[:, :HALF] = masked(0, live_pair, 0, 0)
    first[:, HALF:] = eye
    second[:, :HALF] = masked(2, live_slot, 0, 0)
    second[:, HALF:] = masked(3, live_slot, 0, HALF)

    def half(index, carry):
        eliminate(first, second, turn)

        @pl.when(index == 0)
        def _():
            pair_turn = first[:, HALF:]
            pair_cross = dot(pair_turn, masked(1, live_pair, 0, HALF), 1, 0)
            slot_cross = second[:, HALF:]
            kept[:, :HALF] = pair_turn
            kept[:, HALF : 2 * HALF] = pair_cross
            kept[:, 2 * HALF : 4 * HALF] = second[...]
            first[:, :HALF] = masked(0, live_pair, HALF, HALF) - dot(
                pair_cross, pair_cross, 0, 0
            )
            first[:, HALF:] = eye
            second[:, :HALF] = masked(2, live_slot, HALF, HALF) - dot(
                slot_cross, slot_cross, 0, 0
            )

        return carry

    lax.fori_loop(0, 2, half, 0, unroll=True)

    column_ids = lax.broadcasted_iota(jnp.int32, (1, breadth), 1).astype(jnp.float32)
    site = data_ref[:, :here, :].reshape(peers * here, breadth)
    row_ids = lax.broadcasted_iota(jnp.int32, site.shape, 0)
    alive = jnp.logical_and(row_ids < meta[0], column_ids < live_pair)
    site = jnp.where(alive, site, 0.0)
    full_scale = math.sqrt(4 * peers * here)
    one = product(site[:, :HALF], kept[:, :HALF], 1)
    two = site[:, HALF:] - product(one, kept[:, HALF : 2 * HALF], 0)
    two = product(two, first[:, HALF:], 1)
    out_ref[:, :here, :HALF] = (full_scale * one).reshape(peers, here, HALF)
    out_ref[:, :here, HALF:] = (full_scale * two).reshape(peers, here, HALF)

    squares = jnp.sum(lasts, axis=0, keepdims=True)[:, HALF - 1 :]
    scale = lax.rsqrt(squares * (1.0 / entries) + 1e-06)
    nxt = data_ref[:, here:, :].reshape(peers * STEP, breadth)
    nxt = jnp.where(column_ids < live_slot, nxt, 0.0)
    one = product(nxt[:, :HALF], kept[:, 2 * HALF : 3 * HALF], 1) + product(
        nxt[:, HALF:], kept[:, 3 * HALF :], 1
    )
    two = product(nxt[:, HALF:], second[:, :HALF], 1)
    out_ref[:, here:, :HALF] = (scale * one).reshape(peers, STEP, HALF)
    out_ref[:, here:, HALF:] = (scale * two).reshape(peers, STEP, HALF)


def body(site_blocks, row_lengths, column_lengths, joining, owner_slots, next_blocks):
    sector_count, states, row_count, breadth = site_blocks.shape
    slots, local_columns = next_blocks.shape[:2]
    n_row = lax.axis_size("row")
    n_all = n_row * lax.axis_size("grp")
    both = ("grp", "row")
    quarters = n_row // slots
    piece_columns = local_columns // quarters
    sent = pl.pallas_call(
        gather_kernel,
        out_shape=jax.ShapeDtypeStruct((n_row, row_count + piece_columns, breadth), jnp.float32),
        in_specs=[HBM, HBM],
        out_specs=VMEM,
        scratch_shapes=[pltpu.SemaphoreType.DMA((2,))],
        compiler_params=PARAMS,
        name="gather",
    )(
        pltpu.with_memory_space_constraint(
            site_blocks.reshape(n_row, row_count, breadth), pltpu.HBM
        ),
        pltpu.with_memory_space_constraint(
            next_blocks.reshape(n_row, piece_columns, breadth), pltpu.HBM
        ),
    )

    def swap(x):
        slots_of = x.reshape(n_all, 1, SLOT * HALF)
        return lax.all_to_all(slots_of, both, 0, 0, tiled=True).reshape(x.shape)

    data = lax.all_to_all(sent, "row", 0, 0, tiled=True)
    gram, meta, live, join_row, join_col, owner_col = pl.pallas_call(
        gram_kernel,
        out_shape=(
            jax.ShapeDtypeStruct((n_all * SLOT, HALF), jnp.float32),
            jax.ShapeDtypeStruct((2,), jnp.int32),
            jax.ShapeDtypeStruct((2, HALF), jnp.float32),
            jax.ShapeDtypeStruct((1, n_all), jnp.float32),
            jax.ShapeDtypeStruct((n_all, 1), jnp.float32),
            jax.ShapeDtypeStruct((n_all, 1), jnp.float32),
        ),
        in_specs=[SMEM, SMEM, SMEM, SMEM, VMEM, VMEM, VMEM, VMEM],
        out_specs=(VMEM, SMEM, VMEM, VMEM, VMEM, VMEM),
        compiler_params=PARAMS,
        name="gram",
    )(
        row_lengths,
        column_lengths,
        joining.T,
        owner_slots,
        row_lengths.reshape(1, -1),
        joining.T,
        owner_slots.reshape(1, -1),
        data,
    )
    pieces = swap(gram)
    rows = pl.pallas_call(
        combine_kernel,
        out_shape=jax.ShapeDtypeStruct((n_all * SLOT, HALF), jnp.float32),
        in_specs=[SMEM, VMEM, VMEM, VMEM, VMEM],
        out_specs=VMEM,
        compiler_params=PARAMS,
        name="combine",
    )(meta, join_row, join_col, owner_col, pieces)
    grams = swap(rows)
    entries = float(n_row * local_columns * breadth * slots * lax.axis_size("grp"))
    result = pl.pallas_call(
        functools.partial(apply_kernel, entries),
        out_shape=jax.ShapeDtypeStruct(sent.shape, jnp.float32),
        in_specs=[SMEM, VMEM, VMEM, VMEM],
        out_specs=VMEM,
        scratch_shapes=[
            pltpu.VMEM((HALF, 2 * HALF), jnp.float32),
            pltpu.VMEM((HALF, 2 * HALF), jnp.float32),
            pltpu.VMEM((HALF, 4 * HALF), jnp.float32),
            pltpu.VMEM((2 * STEP, 2 * HALF), jnp.float32),
        ],
        compiler_params=PARAMS,
        name="factor_apply",
    )(meta, live, data, grams)
    back = lax.all_to_all(result, "row", 0, 0, tiled=True)
    canonical, next_site = pl.pallas_call(
        scatter_kernel,
        out_shape=(
            jax.ShapeDtypeStruct((n_row, row_count, breadth), jnp.float32),
            jax.ShapeDtypeStruct((n_row, piece_columns, breadth), jnp.float32),
        ),
        in_specs=[VMEM],
        out_specs=(HBM, HBM),
        scratch_shapes=[pltpu.SemaphoreType.DMA((2,))],
        compiler_params=PARAMS,
        name="scatter",
    )(back)
    canonical = canonical.reshape(site_blocks.shape)
    next_site = next_site.reshape(next_blocks.shape)
    return (canonical, next_site)


def solution(mesh):
    in_specs = (P("grp", None, "row", None), P(), P(), P(), P(), P("grp", "row", None))
    out_specs = (P("grp", None, "row", None), P("grp", "row", None))
    return jax.shard_map(body, mesh=mesh, in_specs=in_specs, out_specs=out_specs, check_vma=False)
```

```python
import functools
import math

import jax
import jax.numpy as jnp
from jax import lax
from jax.experimental import pallas as pl
from jax.experimental.pallas import tpu as pltpu
from jax.sharding import PartitionSpec as P

PRECISE = lax.Precision.HIGHEST
HALF = 128
STEP = 8
SLOT = 5
WHEN = 4
HBM = pl.BlockSpec(memory_space=pltpu.HBM)
PARAMS = pltpu.CompilerParams(vmem_limit_bytes=16 * 1024 * 1024)
VMEM = pl.BlockSpec(memory_space=pltpu.VMEM)
SMEM = pl.BlockSpec(memory_space=pltpu.SMEM)


def dot(a, b, ca, cb):
    return lax.dot_general(
        a, b, (((ca,), (cb,)), ((), ())), precision=PRECISE, preferred_element_type=jnp.float32
    )


def gather_kernel(site_ref, next_ref, *refs):
    tables, out_ref, held, sems = refs[:4], refs[4], refs[5:9], refs[9]
    here = site_ref.shape[1]
    copies = [
        pltpu.make_async_copy(site_ref, out_ref.at[:, :here, :], sems.at[0]),
        pltpu.make_async_copy(next_ref, out_ref.at[:, here:, :], sems.at[1]),
    ]
    for i in range(4):
        copies.append(pltpu.make_async_copy(tables[i], held[i], sems.at[2 + i]))
    for copy in copies:
        copy.start()
    for copy in copies:
        copy.wait()


def scatter_kernel(data_ref, site_ref, next_ref, sems):
    here = site_ref.shape[1]
    one = pltpu.make_async_copy(data_ref.at[:, :here, :], site_ref, sems.at[0])
    two = pltpu.make_async_copy(data_ref.at[:, here:, :], next_ref, sems.at[1])
    one.start()
    two.start()
    one.wait()
    two.wait()


def slot_rows(index):
    return pl.ds(index, HALF, stride=SLOT)


def split(x):
    high = x.astype(jnp.bfloat16).astype(jnp.float32)
    rest = x - high
    middle = rest.astype(jnp.bfloat16).astype(jnp.float32)
    return high, middle, rest - middle


def gram_kernel(
    row_lengths,
    column_lengths,
    joining,
    owner_slots,
    rows_ref,
    join_ref,
    owner_ref,
    data_ref,
    out_ref,
    meta_ref,
    live_ref,
    join_row,
    join_col,
    owner_col,
):
    states, sectors = join_ref.shape
    n_row = lax.axis_size("row")
    group, place = lax.axis_index("grp"), lax.axis_index("row")
    left = group * (n_row // states) + place // states
    meta_ref[0] = row_lengths[0, left]
    meta_ref[1] = group * n_row + place
    joins = join_ref[...]
    for index, sector in enumerate((joining[place % states, left], owner_slots[0, left])):
        joined = jnp.sum(jnp.where(joins == sector, rows_ref[...], 0), axis=0, keepdims=True)
        joined = jnp.sum(joined.astype(jnp.float32), axis=1, keepdims=True)
        live = jnp.minimum(jnp.floor(joined * 0.5), column_lengths[0, sector].astype(jnp.float32))
        live_ref[index : index + 1, :] = jnp.broadcast_to(live, (1, HALF))
    lefts = lax.broadcasted_iota(jnp.int32, (sectors, HALF), 0)
    devices = lax.broadcasted_iota(jnp.int32, (sectors, HALF), 1)
    expand = (devices // states == lefts).astype(jnp.float32)
    by_state = dot(joins.astype(jnp.float32), expand, 1, 0)
    state = lax.broadcasted_iota(jnp.int32, (states, HALF), 0)
    device = lax.broadcasted_iota(jnp.int32, (states, HALF), 1)
    row = jnp.sum(jnp.where(device % states == state, by_state, 0.0), axis=0, keepdims=True)
    owners = dot(owner_ref[...].astype(jnp.float32), expand, 1, 0)
    join_row[...] = row
    sub = lax.broadcasted_iota(jnp.int32, (HALF, HALF), 0)
    lane = lax.broadcasted_iota(jnp.int32, (HALF, HALF), 1)
    join_col[...] = jnp.sum(jnp.where(sub == lane, row, 0.0), axis=1, keepdims=True)
    owner_col[...] = jnp.sum(jnp.where(sub == lane, owners, 0.0), axis=1, keepdims=True)
    peers, depth, breadth = data_ref.shape
    here = depth - STEP
    site = data_ref[:, :here, :].reshape(peers * here, breadth)
    row_ids = lax.broadcasted_iota(jnp.int32, site.shape, 0)
    site = jnp.where(row_ids < row_lengths[0, left], site, 0.0)
    nxt = data_ref[:, here:, :].reshape(peers * STEP, breadth)
    live_slot = live
    column_ids = lax.broadcasted_iota(jnp.int32, (1, breadth), 1).astype(jnp.float32)
    nxt = jnp.where(column_ids < live_slot, nxt, 0.0)
    sub = lax.broadcasted_iota(jnp.int32, (HALF, HALF), 0)
    lane = lax.broadcasted_iota(jnp.int32, (HALF, HALF), 1)
    diagonals = []
    for start, block in ((0, site), (2, nxt)):
        high, middle, low = (part.astype(jnp.bfloat16) for part in split(block))
        dims = (((0,), (0,)), ((), ()))
        wide = lax.dot_general(high, middle, dims, preferred_element_type=jnp.float32)
        wide = wide + lax.dot_general(high, low, dims, preferred_element_type=jnp.float32)
        square = lax.dot_general(high, high, dims, preferred_element_type=jnp.float32)
        square = square + lax.dot_general(middle, middle, dims, preferred_element_type=jnp.float32)
        square = square + (wide + wide.T)
        top, low = square[:HALF], square[HALF:, HALF:]
        out_ref[slot_rows(start), :] = jnp.where(sub <= lane, top[:, :HALF], low)
        out_ref[slot_rows(start + 1), :] = top[:, HALF:]
        diagonals.append(jnp.sum(jnp.where(sub == lane, low, 0.0), axis=1, keepdims=True))
    out_ref[slot_rows(4), :] = jnp.where(lane < HALF // 2, diagonals[0], diagonals[1])


def combine_kernel(meta, join_row, join_col, owner_col, piece_ref, out_ref):
    packed, cross, diagonal = (slice(i * HALF, (i + 1) * HALF) for i in range(3))
    piece = jnp.concatenate([piece_ref[slot_rows(i), :] for i in (0, 1, 4)], axis=1)
    hot = jnp.concatenate([join_col[...] == join_row[...], owner_col[...] == join_row[...]], axis=0)
    hot = hot.astype(jnp.float32).astype(jnp.bfloat16)
    parts = 0.0
    for part in split(piece)[::-1]:
        parts = parts + lax.dot_general(
            hot,
            part.astype(jnp.bfloat16),
            (((1,), (0,)), ((), ())),
            preferred_element_type=jnp.float32,
        )
    pair_part, slot_part = parts[:HALF], parts[HALF:]
    out_ref[slot_rows(0), :] = pair_part[:, packed]
    out_ref[slot_rows(1), :] = pair_part[:, cross]
    out_ref[slot_rows(2), :] = slot_part[:, packed]
    out_ref[slot_rows(3), :] = slot_part[:, cross]
    lane = lax.broadcasted_iota(jnp.int32, (1, HALF), 1)
    norm = jnp.where(lane == meta[1], 1.0, 2.0) * slot_part[:, packed] * piece_ref[slot_rows(2), :]
    norm = norm + 2.0 * slot_part[:, cross] * piece_ref[slot_rows(3), :]
    moment = jnp.where(lane == HALF - 1, pltpu.roll(slot_part[:, diagonal], HALF // 2, 1), 0.0)
    norm = norm + moment * piece_ref[slot_rows(4), :]
    norm = jnp.sum(jnp.sum(norm, axis=0, keepdims=True), axis=1, keepdims=True)
    quarter = HALF // 4
    pair_diagonal = jnp.broadcast_to(pair_part[:, 2 * HALF : 2 * HALF + 1], (HALF, HALF))
    slot_diagonal = jnp.broadcast_to(slot_part[:, 2 * HALF : 2 * HALF + 1], (HALF, HALF))
    last = jnp.where(lane < quarter, pair_diagonal, slot_diagonal)
    out_ref[slot_rows(4), :] = jnp.where(lane < 2 * quarter, last, norm)


def product(x, w, contract):
    parts = [p.astype(jnp.bfloat16) for p in split(x)]
    high, middle, low = (p.astype(jnp.bfloat16) for p in split(w))
    wide = jnp.concatenate([parts[0], parts[1]], axis=1)
    tall = jnp.concatenate([parts[0], parts[2]], axis=1)
    inner, outer = contract, 1 - contract
    one = jnp.concatenate(
        [jnp.concatenate([p, p], axis=inner) for p in (high, middle)], axis=outer
    )
    two = jnp.concatenate([low, high], axis=inner)
    dims = (((1,), (inner,)), ((), ()))
    main = lax.dot_general(wide, one, dims, preferred_element_type=jnp.float32)
    rest = lax.dot_general(tall, two, dims, preferred_element_type=jnp.float32)
    width = w.shape[outer]
    return main[:, :width] + (main[:, width:] + rest)


def eliminate(first, second, turn):
    shape = (STEP, HALF)
    sub = lax.broadcasted_iota(jnp.int32, shape, 0)
    lane = lax.broadcasted_iota(jnp.int32, shape, 1)
    upper_half = sub < STEP // 2

    def load(row, side):
        cut = slice(side * HALF, (side + 1) * HALF)
        one = jnp.broadcast_to(first[row : row + 1, cut], shape)
        two = jnp.broadcast_to(second[row : row + 1, cut], shape)
        return jnp.where(upper_half, one, two)

    def spread(x, column):
        return jnp.broadcast_to(x[:, column : column + 1], shape)

    def finish(start, sides):
        after = start + STEP
        panels = [[], []]
        for rows in sides:
            straight, crossed = rows[0], rows[STEP // 2]
            for k in range(1, STEP):
                straight = jnp.where(sub == k, rows[k], straight)
                crossed = jnp.where(sub == k, rows[(k + STEP // 2) % STEP], crossed)
            crossed = pltpu.roll(crossed, STEP // 2, 0)
            panels[0].append(jnp.where(upper_half, straight, crossed))
            panels[1].append(jnp.where(upper_half, crossed, straight))
        for work_ref, (one, two) in zip((first, second), panels):
            one = jnp.where(lane >= sub + start, one, 0.0)
            panel = jnp.concatenate([one, two], axis=1)
            work_ref[start:after, :] = panel
            if after + STEP < HALF:
                high, middle, low = split(panel)
                lhs = jnp.concatenate([high, high, middle, middle, high, low], axis=0)[:, :HALF]
                rhs = jnp.concatenate([high, middle, high, middle, low, high], axis=0)
                base = (after + STEP) // 16 * 16
                update = lax.dot_general(
                    lhs.astype(jnp.bfloat16).T[base:],
                    rhs.astype(jnp.bfloat16),
                    (((1,), (0,)), ((), ())),
                    preferred_element_type=jnp.float32,
                )
                rest = slice(after + STEP, HALF)
                work_ref[rest, :] = work_ref[rest, :] - update[after + STEP - base :, :]

    quad = STEP // 2
    sides = [[load(i, side) for i in range(STEP)] for side in (0, 1)]
    done = None
    for start in range(0, HALF, STEP):
        after = start + STEP
        a = [[spread(sides[0][i], start + j) for i in range(j + 1)] for j in range(STEP)]
        following = None
        for k in range(STEP):
            root = lax.rsqrt(a[k][k])
            for j in range(k + 1, STEP):
                a[j][k] = a[j][k] * root
            for j in range(k + 1, STEP):
                for i in range(k + 1, j + 1):
                    a[j][i] = a[j][i] - a[j][k] * a[i][k]
            for rows in sides:
                rows[k] = rows[k] * root
                for j in range(k + 1, STEP):
                    rows[j] = rows[j] - a[j][k] * rows[k]
            if k == WHEN and done is not None:
                finish(*done)
            if after < HALF:
                if following is None:
                    totals = [[None, None], [None, None]]
                    following = True
                for part in (0, 1):
                    index = after + part * quad + sub % quad
                    factor = jnp.take_along_axis(sides[0][k], index, axis=1)
                    for rows, total in zip(sides, totals):
                        term = factor * rows[k]
                        total[part] = term if k == 0 else total[part] + term
        done = (start, sides)
        if after < HALF:
            for side in (0, 1):
                cut = slice(side * HALF, (side + 1) * HALF)
                one, two = first[after : after + STEP, cut], second[after : after + STEP, cut]
                early = jnp.where(upper_half, one, pltpu.roll(two, quad, 0))
                late = jnp.where(upper_half, pltpu.roll(one, quad, 0), two)
                turn[:STEP, cut] = early - totals[side][0]
                turn[STEP:, cut] = late - totals[side][1]

            def reload(i, side):
                cut = slice(side * HALF, (side + 1) * HALF)
                row = i // quad * STEP + i % quad
                one = jnp.broadcast_to(turn[row : row + 1, cut], shape)
                two = jnp.broadcast_to(turn[row + quad : row + quad + 1, cut], shape)
                return jnp.where(upper_half, one, two)

            sides = [[reload(i, side) for i in range(STEP)] for side in (0, 1)]
    finish(*done)


def apply_kernel(
    entries, meta, live_ref, data_ref, gram_ref, out_ref, first, second, kept, turn
):
    peers, depth, breadth = data_ref.shape
    here = depth - STEP
    live_pair = live_ref[:1, :1]
    live_slot = live_ref[1:2, :1]
    sub = lax.broadcasted_iota(jnp.int32, (HALF, HALF), 0)
    lane = lax.broadcasted_iota(jnp.int32, (HALF, HALF), 1)
    eye = jnp.where(sub == lane, 1.0, 0.0)
    sub = sub.astype(jnp.float32)
    lane = lane.astype(jnp.float32)

    lasts = gram_ref[slot_rows(4), :]

    def masked(start, live, row_from, col_from):
        block = gram_ref[slot_rows(start), :]
        if row_from:
            column = start * HALF // 8
            block = jnp.where(sub == lane, lasts[:, column : column + 1], block.T)
        alive = jnp.logical_and(sub + row_from < live, lane + col_from < live)
        return jnp.where(alive, block, eye if row_from == col_from else 0.0)

    first[:, :HALF] = masked(0, live_pair, 0, 0)
    first[:, HALF:] = eye
    second[:, :HALF] = masked(2, live_slot, 0, 0)
    second[:, HALF:] = masked(3, live_slot, 0, HALF)

    def half(index, carry):
        eliminate(first, second, turn)

        @pl.when(index == 0)
        def _():
            pair_turn = first[:, HALF:]
            pair_cross = dot(pair_turn, masked(1, live_pair, 0, HALF), 1, 0)
            slot_cross = second[:, HALF:]
            kept[:, :HALF] = pair_turn
            kept[:, HALF : 2 * HALF] = pair_cross
            kept[:, 2 * HALF : 4 * HALF] = second[...]
            first[:, :HALF] = masked(0, live_pair, HALF, HALF) - dot(
                pair_cross, pair_cross, 0, 0
            )
            first[:, HALF:] = eye
            second[:, :HALF] = masked(2, live_slot, HALF, HALF) - dot(
                slot_cross, slot_cross, 0, 0
            )

        return carry

    lax.fori_loop(0, 2, half, 0, unroll=True)

    column_ids = lax.broadcasted_iota(jnp.int32, (1, breadth), 1).astype(jnp.float32)
    site = data_ref[:, :here, :].reshape(peers * here, breadth)
    row_ids = lax.broadcasted_iota(jnp.int32, site.shape, 0)
    alive = jnp.logical_and(row_ids < meta[0], column_ids < live_pair)
    site = jnp.where(alive, site, 0.0)
    full_scale = math.sqrt(4 * peers * here)
    one = product(site[:, :HALF], kept[:, :HALF], 1)
    two = site[:, HALF:] - product(one, kept[:, HALF : 2 * HALF], 0)
    two = product(two, first[:, HALF:], 1)
    out_ref[:, :here, :HALF] = (full_scale * one).reshape(peers, here, HALF)
    out_ref[:, :here, HALF:] = (full_scale * two).reshape(peers, here, HALF)

    squares = jnp.sum(lasts, axis=0, keepdims=True)[:, HALF - 1 :]
    scale = lax.rsqrt(squares * (1.0 / entries) + 1e-06)
    nxt = data_ref[:, here:, :].reshape(peers * STEP, breadth)
    nxt = jnp.where(column_ids < live_slot, nxt, 0.0)
    one = product(nxt[:, :HALF], kept[:, 2 * HALF : 3 * HALF], 1) + product(
        nxt[:, HALF:], kept[:, 3 * HALF :], 1
    )
    two = product(nxt[:, HALF:], second[:, :HALF], 1)
    out_ref[:, here:, :HALF] = (scale * one).reshape(peers, STEP, HALF)
    out_ref[:, here:, HALF:] = (scale * two).reshape(peers, STEP, HALF)


def body(site_blocks, row_lengths, column_lengths, joining, owner_slots, next_blocks):
    sector_count, states, row_count, breadth = site_blocks.shape
    slots, local_columns = next_blocks.shape[:2]
    n_row = lax.axis_size("row")
    n_all = n_row * lax.axis_size("grp")
    both = ("grp", "row")
    quarters = n_row // slots
    piece_columns = local_columns // quarters
    tables = (
        row_lengths.reshape(1, -1),
        column_lengths.reshape(1, -1),
        joining.T,
        owner_slots.reshape(1, -1),
    )
    arrays = (
        site_blocks.reshape(n_row, row_count, breadth),
        next_blocks.reshape(n_row, piece_columns, breadth),
    ) + tables
    sent, rows_line, columns_line, joins, owner_line = pl.pallas_call(
        gather_kernel,
        out_shape=(
            jax.ShapeDtypeStruct((n_row, row_count + piece_columns, breadth), jnp.float32),
        )
        + tuple(jax.ShapeDtypeStruct(t.shape, t.dtype) for t in tables),
        in_specs=[HBM] * 6,
        out_specs=(VMEM,) * 5,
        scratch_shapes=[pltpu.SemaphoreType.DMA((6,))],
        compiler_params=PARAMS,
        name="gather",
    )(*(pltpu.with_memory_space_constraint(x, pltpu.HBM) for x in arrays))

    def swap(x):
        slots_of = x.reshape(n_all, 1, SLOT * HALF)
        return lax.all_to_all(slots_of, both, 0, 0, tiled=True).reshape(x.shape)

    data = lax.all_to_all(sent, "row", 0, 0, tiled=True)
    gram, meta, live, join_row, join_col, owner_col = pl.pallas_call(
        gram_kernel,
        out_shape=(
            jax.ShapeDtypeStruct((n_all * SLOT, HALF), jnp.float32),
            jax.ShapeDtypeStruct((2,), jnp.int32),
            jax.ShapeDtypeStruct((2, HALF), jnp.float32),
            jax.ShapeDtypeStruct((1, n_all), jnp.float32),
            jax.ShapeDtypeStruct((n_all, 1), jnp.float32),
            jax.ShapeDtypeStruct((n_all, 1), jnp.float32),
        ),
        in_specs=[SMEM, SMEM, SMEM, SMEM, VMEM, VMEM, VMEM, VMEM],
        out_specs=(VMEM, SMEM, VMEM, VMEM, VMEM, VMEM),
        compiler_params=PARAMS,
        name="gram",
    )(
        rows_line,
        columns_line,
        joins,
        owner_line,
        rows_line,
        joins,
        owner_line,
        data,
    )
    pieces = swap(gram)
    rows = pl.pallas_call(
        combine_kernel,
        out_shape=jax.ShapeDtypeStruct((n_all * SLOT, HALF), jnp.float32),
        in_specs=[SMEM, VMEM, VMEM, VMEM, VMEM],
        out_specs=VMEM,
        compiler_params=PARAMS,
        name="combine",
    )(meta, join_row, join_col, owner_col, pieces)
    grams = swap(rows)
    entries = float(n_row * local_columns * breadth * slots * lax.axis_size("grp"))
    result = pl.pallas_call(
        functools.partial(apply_kernel, entries),
        out_shape=jax.ShapeDtypeStruct(sent.shape, jnp.float32),
        in_specs=[SMEM, VMEM, VMEM, VMEM],
        out_specs=VMEM,
        scratch_shapes=[
            pltpu.VMEM((HALF, 2 * HALF), jnp.float32),
            pltpu.VMEM((HALF, 2 * HALF), jnp.float32),
            pltpu.VMEM((HALF, 4 * HALF), jnp.float32),
            pltpu.VMEM((2 * STEP, 2 * HALF), jnp.float32),
        ],
        compiler_params=PARAMS,
        name="factor_apply",
    )(meta, live, data, grams)
    back = lax.all_to_all(result, "row", 0, 0, tiled=True)
    canonical, next_site = pl.pallas_call(
        scatter_kernel,
        out_shape=(
            jax.ShapeDtypeStruct((n_row, row_count, breadth), jnp.float32),
            jax.ShapeDtypeStruct((n_row, piece_columns, breadth), jnp.float32),
        ),
        in_specs=[VMEM],
        out_specs=(HBM, HBM),
        scratch_shapes=[pltpu.SemaphoreType.DMA((2,))],
        compiler_params=PARAMS,
        name="scatter",
    )(back)
    canonical = canonical.reshape(site_blocks.shape)
    next_site = next_site.reshape(next_blocks.shape)
    return (canonical, next_site)


def solution(mesh):
    in_specs = (P("grp", None, "row", None), P(), P(), P(), P(), P("grp", "row", None))
    out_specs = (P("grp", None, "row", None), P("grp", "row", None))
    return jax.shard_map(body, mesh=mesh, in_specs=in_specs, out_specs=out_specs, check_vma=False)
```

```python
import functools
import math

import jax
import jax.numpy as jnp
from jax import lax
from jax.experimental import pallas as pl
from jax.experimental.pallas import tpu as pltpu
from jax.sharding import PartitionSpec as P

PRECISE = lax.Precision.HIGHEST
HALF = 128
STEP = 8
SLOT = 5
WHEN = 4
HBM = pl.BlockSpec(memory_space=pltpu.HBM)
PARAMS = pltpu.CompilerParams(vmem_limit_bytes=16 * 1024 * 1024)
VMEM = pl.BlockSpec(memory_space=pltpu.VMEM)
SMEM = pl.BlockSpec(memory_space=pltpu.SMEM)


def dot(a, b, ca, cb):
    return lax.dot_general(
        a, b, (((ca,), (cb,)), ((), ())), precision=PRECISE, preferred_element_type=jnp.float32
    )


def gather_kernel(site_ref, next_ref, *refs):
    tables, out_ref, held, sems = refs[:4], refs[4], refs[5:9], refs[9]
    here = site_ref.shape[1]
    copies = [
        pltpu.make_async_copy(site_ref, out_ref.at[:, :here, :], sems.at[0]),
        pltpu.make_async_copy(next_ref, out_ref.at[:, here:, :], sems.at[1]),
    ]
    for i in range(4):
        copies.append(pltpu.make_async_copy(tables[i], held[i], sems.at[2 + i]))
    for copy in copies:
        copy.start()
    for copy in copies:
        copy.wait()


def scatter_kernel(data_ref, site_ref, next_ref, sems):
    here = site_ref.shape[1]
    one = pltpu.make_async_copy(data_ref.at[:, :here, :], site_ref, sems.at[0])
    two = pltpu.make_async_copy(data_ref.at[:, here:, :], next_ref, sems.at[1])
    one.start()
    two.start()
    one.wait()
    two.wait()


def slot_rows(index):
    return pl.ds(index, HALF, stride=SLOT)


def split(x):
    high = x.astype(jnp.bfloat16).astype(jnp.float32)
    rest = x - high
    middle = rest.astype(jnp.bfloat16).astype(jnp.float32)
    return high, middle, rest - middle


def gram_kernel(
    row_lengths,
    column_lengths,
    joining,
    owner_slots,
    rows_ref,
    join_ref,
    owner_ref,
    data_ref,
    out_ref,
    meta_ref,
    live_ref,
    join_row,
    join_col,
    owner_col,
):
    states, sectors = join_ref.shape
    n_row = lax.axis_size("row")
    group, place = lax.axis_index("grp"), lax.axis_index("row")
    left = group * (n_row // states) + place // states
    meta_ref[0] = row_lengths[0, left]
    meta_ref[1] = group * n_row + place
    joins = join_ref[...]
    for index, sector in enumerate((joining[place % states, left], owner_slots[0, left])):
        joined = jnp.sum(jnp.where(joins == sector, rows_ref[...], 0), axis=0, keepdims=True)
        joined = jnp.sum(joined.astype(jnp.float32), axis=1, keepdims=True)
        live = jnp.minimum(jnp.floor(joined * 0.5), column_lengths[0, sector].astype(jnp.float32))
        live_ref[index : index + 1, :] = jnp.broadcast_to(live, (1, HALF))
    lefts = lax.broadcasted_iota(jnp.int32, (sectors, HALF), 0)
    devices = lax.broadcasted_iota(jnp.int32, (sectors, HALF), 1)
    expand = (devices // states == lefts).astype(jnp.float32)
    by_state = dot(joins.astype(jnp.float32), expand, 1, 0)
    state = lax.broadcasted_iota(jnp.int32, (states, HALF), 0)
    device = lax.broadcasted_iota(jnp.int32, (states, HALF), 1)
    row = jnp.sum(jnp.where(device % states == state, by_state, 0.0), axis=0, keepdims=True)
    owners = dot(owner_ref[...].astype(jnp.float32), expand, 1, 0)
    join_row[...] = row
    sub = lax.broadcasted_iota(jnp.int32, (HALF, HALF), 0)
    lane = lax.broadcasted_iota(jnp.int32, (HALF, HALF), 1)
    join_col[...] = jnp.sum(jnp.where(sub == lane, row, 0.0), axis=1, keepdims=True)
    owner_col[...] = jnp.sum(jnp.where(sub == lane, owners, 0.0), axis=1, keepdims=True)
    peers, depth, breadth = data_ref.shape
    here = depth - STEP
    site = data_ref[:, :here, :].reshape(peers * here, breadth)
    row_ids = lax.broadcasted_iota(jnp.int32, site.shape, 0)
    site = jnp.where(row_ids < row_lengths[0, left], site, 0.0)
    nxt = data_ref[:, here:, :].reshape(peers * STEP, breadth)
    live_slot = live
    column_ids = lax.broadcasted_iota(jnp.int32, (1, breadth), 1).astype(jnp.float32)
    nxt = jnp.where(column_ids < live_slot, nxt, 0.0)
    sub = lax.broadcasted_iota(jnp.int32, (HALF, HALF), 0)
    lane = lax.broadcasted_iota(jnp.int32, (HALF, HALF), 1)
    diagonals = []
    for start, block in ((0, site), (2, nxt)):
        high, middle, low = (part.astype(jnp.bfloat16) for part in split(block))
        dims = (((0,), (0,)), ((), ()))
        wide = lax.dot_general(high, middle, dims, preferred_element_type=jnp.float32)
        wide = wide + lax.dot_general(high, low, dims, preferred_element_type=jnp.float32)
        square = lax.dot_general(high, high, dims, preferred_element_type=jnp.float32)
        square = square + lax.dot_general(middle, middle, dims, preferred_element_type=jnp.float32)
        square = square + (wide + wide.T)
        top, low = square[:HALF], square[HALF:, HALF:]
        out_ref[slot_rows(start), :] = jnp.where(sub <= lane, top[:, :HALF], low)
        out_ref[slot_rows(start + 1), :] = top[:, HALF:]
        diagonals.append(jnp.sum(jnp.where(sub == lane, low, 0.0), axis=1, keepdims=True))
    out_ref[slot_rows(4), :] = jnp.where(lane < HALF // 2, diagonals[0], diagonals[1])


def combine_kernel(meta, join_row, join_col, owner_col, piece_ref, out_ref):
    packed, cross, diagonal = (slice(i * HALF, (i + 1) * HALF) for i in range(3))
    piece = jnp.concatenate([piece_ref[slot_rows(i), :] for i in (0, 1, 4)], axis=1)
    hot = jnp.concatenate([join_col[...] == join_row[...], owner_col[...] == join_row[...]], axis=0)
    hot = hot.astype(jnp.float32).astype(jnp.bfloat16)
    parts = 0.0
    for part in split(piece)[::-1]:
        parts = parts + lax.dot_general(
            hot,
            part.astype(jnp.bfloat16),
            (((1,), (0,)), ((), ())),
            preferred_element_type=jnp.float32,
        )
    pair_part, slot_part = parts[:HALF], parts[HALF:]
    out_ref[slot_rows(0), :] = pair_part[:, packed]
    out_ref[slot_rows(1), :] = pair_part[:, cross]
    out_ref[slot_rows(2), :] = slot_part[:, packed]
    out_ref[slot_rows(3), :] = slot_part[:, cross]
    lane = lax.broadcasted_iota(jnp.int32, (1, HALF), 1)
    norm = jnp.where(lane == meta[1], 1.0, 2.0) * slot_part[:, packed] * piece_ref[slot_rows(2), :]
    norm = norm + 2.0 * slot_part[:, cross] * piece_ref[slot_rows(3), :]
    moment = jnp.where(lane == HALF - 1, pltpu.roll(slot_part[:, diagonal], HALF // 2, 1), 0.0)
    norm = norm + moment * piece_ref[slot_rows(4), :]
    norm = jnp.sum(jnp.sum(norm, axis=0, keepdims=True), axis=1, keepdims=True)
    quarter = HALF // 4
    pair_diagonal = jnp.broadcast_to(pair_part[:, 2 * HALF : 2 * HALF + 1], (HALF, HALF))
    slot_diagonal = jnp.broadcast_to(slot_part[:, 2 * HALF : 2 * HALF + 1], (HALF, HALF))
    last = jnp.where(lane < quarter, pair_diagonal, slot_diagonal)
    out_ref[slot_rows(4), :] = jnp.where(lane < 2 * quarter, last, norm)


def product(x, w, contract):
    parts = [p.astype(jnp.bfloat16) for p in split(x)]
    high, middle, low = (p.astype(jnp.bfloat16) for p in split(w))
    wide = jnp.concatenate([parts[0], parts[1]], axis=1)
    tall = jnp.concatenate([parts[0], parts[2]], axis=1)
    inner, outer = contract, 1 - contract
    one = jnp.concatenate(
        [jnp.concatenate([p, p], axis=inner) for p in (high, middle)], axis=outer
    )
    two = jnp.concatenate([low, high], axis=inner)
    dims = (((1,), (inner,)), ((), ()))
    main = lax.dot_general(wide, one, dims, preferred_element_type=jnp.float32)
    rest = lax.dot_general(tall, two, dims, preferred_element_type=jnp.float32)
    width = w.shape[outer]
    return main[:, :width] + (main[:, width:] + rest)


def eliminate(first, second, turn):
    shape = (STEP, HALF)
    sub = lax.broadcasted_iota(jnp.int32, shape, 0)
    lane = lax.broadcasted_iota(jnp.int32, shape, 1)
    upper_half = sub < STEP // 2

    def load(row, side):
        cut = slice(side * HALF, (side + 1) * HALF)
        one = jnp.broadcast_to(first[row : row + 1, cut], shape)
        two = jnp.broadcast_to(second[row : row + 1, cut], shape)
        return jnp.where(upper_half, one, two)

    def spread(x, column):
        return jnp.broadcast_to(x[:, column : column + 1], shape)

    def finish(start, sides):
        after = start + STEP
        panels = [[], []]
        for rows in sides:
            straight, crossed = rows[0], rows[STEP // 2]
            for k in range(1, STEP):
                straight = jnp.where(sub == k, rows[k], straight)
                crossed = jnp.where(sub == k, rows[(k + STEP // 2) % STEP], crossed)
            crossed = pltpu.roll(crossed, STEP // 2, 0)
            panels[0].append(jnp.where(upper_half, straight, crossed))
            panels[1].append(jnp.where(upper_half, crossed, straight))
        for work_ref, (one, two) in zip((first, second), panels):
            one = jnp.where(lane >= sub + start, one, 0.0)
            panel = jnp.concatenate([one, two], axis=1)
            work_ref[start:after, :] = panel
            if after + STEP < HALF:
                high, middle, low = split(panel)
                lhs = jnp.concatenate([high, high, middle, middle, high, low], axis=0)[:, :HALF]
                rhs = jnp.concatenate([high, middle, high, middle, low, high], axis=0)
                base = (after + STEP) // 16 * 16
                update = lax.dot_general(
                    lhs.astype(jnp.bfloat16).T[base:],
                    rhs.astype(jnp.bfloat16),
                    (((1,), (0,)), ((), ())),
                    preferred_element_type=jnp.float32,
                )
                rest = slice(after + STEP, HALF)
                work_ref[rest, :] = work_ref[rest, :] - update[after + STEP - base :, :]

    quad = STEP // 2
    sides = [[load(i, side) for i in range(STEP)] for side in (0, 1)]
    done = None
    for start in range(0, HALF, STEP):
        after = start + STEP
        a = [[spread(sides[0][i], start + j) for i in range(j + 1)] for j in range(STEP)]
        following = None
        for k in range(STEP):
            root = lax.rsqrt(a[k][k])
            for j in range(k + 1, STEP):
                a[j][k] = a[j][k] * root
            for j in range(k + 1, STEP):
                for i in range(k + 1, j + 1):
                    a[j][i] = a[j][i] - a[j][k] * a[i][k]
            for rows in sides:
                rows[k] = rows[k] * root
                for j in range(k + 1, STEP):
                    rows[j] = rows[j] - a[j][k] * rows[k]
            if k == WHEN and done is not None:
                finish(*done)
            if after < HALF:
                if following is None:
                    totals = [[None, None], [None, None]]
                    following = True
                for part in (0, 1):
                    index = after + part * quad + sub % quad
                    factor = jnp.take_along_axis(sides[0][k], index, axis=1)
                    for rows, total in zip(sides, totals):
                        term = factor * rows[k]
                        total[part] = term if k == 0 else total[part] + term
        done = (start, sides)
        if after < HALF:
            for side in (0, 1):
                cut = slice(side * HALF, (side + 1) * HALF)
                one, two = first[after : after + STEP, cut], second[after : after + STEP, cut]
                early = jnp.where(upper_half, one, pltpu.roll(two, quad, 0))
                late = jnp.where(upper_half, pltpu.roll(one, quad, 0), two)
                turn[:STEP, cut] = early - totals[side][0]
                turn[STEP:, cut] = late - totals[side][1]

            def reload(i, side):
                cut = slice(side * HALF, (side + 1) * HALF)
                row = i // quad * STEP + i % quad
                one = jnp.broadcast_to(turn[row : row + 1, cut], shape)
                two = jnp.broadcast_to(turn[row + quad : row + quad + 1, cut], shape)
                return jnp.where(upper_half, one, two)

            sides = [[reload(i, side) for i in range(STEP)] for side in (0, 1)]
    finish(*done)


def apply_kernel(
    entries, meta, live_ref, data_ref, gram_ref, out_ref, first, second, kept, turn
):
    peers, depth, breadth = data_ref.shape
    here = depth - STEP
    live_pair = live_ref[:1, :1]
    live_slot = live_ref[1:2, :1]
    sub = lax.broadcasted_iota(jnp.int32, (HALF, HALF), 0)
    lane = lax.broadcasted_iota(jnp.int32, (HALF, HALF), 1)
    eye = jnp.where(sub == lane, 1.0, 0.0)
    sub = sub.astype(jnp.float32)
    lane = lane.astype(jnp.float32)

    lasts = gram_ref[slot_rows(4), :]

    def masked(start, live, row_from, col_from):
        block = gram_ref[slot_rows(start), :]
        if row_from:
            column = start * HALF // 8
            block = jnp.where(sub == lane, lasts[:, column : column + 1], block.T)
        alive = jnp.logical_and(sub + row_from < live, lane + col_from < live)
        return jnp.where(alive, block, eye if row_from == col_from else 0.0)

    first[:, :HALF] = masked(0, live_pair, 0, 0)
    first[:, HALF:] = eye
    second[:, :HALF] = masked(2, live_slot, 0, 0)
    second[:, HALF:] = masked(3, live_slot, 0, HALF)

    def half(index, carry):
        eliminate(first, second, turn)

        @pl.when(index == 0)
        def _():
            pair_turn = first[:, HALF:]
            pair_cross = product(pair_turn, masked(1, live_pair, 0, HALF), 0)
            slot_cross = second[:, HALF:]
            kept[:, :HALF] = pair_turn
            kept[:, HALF : 2 * HALF] = pair_cross
            kept[:, 2 * HALF : 4 * HALF] = second[...]
            first[:, :HALF] = masked(0, live_pair, HALF, HALF) - dot(
                pair_cross, pair_cross, 0, 0
            )
            first[:, HALF:] = eye
            second[:, :HALF] = masked(2, live_slot, HALF, HALF) - dot(
                slot_cross, slot_cross, 0, 0
            )

        return carry

    lax.fori_loop(0, 2, half, 0, unroll=True)

    column_ids = lax.broadcasted_iota(jnp.int32, (1, breadth), 1).astype(jnp.float32)
    site = data_ref[:, :here, :].reshape(peers * here, breadth)
    row_ids = lax.broadcasted_iota(jnp.int32, site.shape, 0)
    alive = jnp.logical_and(row_ids < meta[0], column_ids < live_pair)
    site = jnp.where(alive, site, 0.0)
    full_scale = math.sqrt(4 * peers * here)
    one = product(site[:, :HALF], kept[:, :HALF], 1)
    two = site[:, HALF:] - product(one, kept[:, HALF : 2 * HALF], 0)
    two = product(two, first[:, HALF:], 1)
    out_ref[:, :here, :HALF] = (full_scale * one).reshape(peers, here, HALF)
    out_ref[:, :here, HALF:] = (full_scale * two).reshape(peers, here, HALF)

    squares = jnp.sum(lasts, axis=0, keepdims=True)[:, HALF - 1 :]
    scale = lax.rsqrt(squares * (1.0 / entries) + 1e-06)
    nxt = data_ref[:, here:, :].reshape(peers * STEP, breadth)
    nxt = jnp.where(column_ids < live_slot, nxt, 0.0)
    one = product(nxt[:, :HALF], kept[:, 2 * HALF : 3 * HALF], 1) + product(
        nxt[:, HALF:], kept[:, 3 * HALF :], 1
    )
    two = product(nxt[:, HALF:], second[:, :HALF], 1)
    out_ref[:, here:, :HALF] = (scale * one).reshape(peers, STEP, HALF)
    out_ref[:, here:, HALF:] = (scale * two).reshape(peers, STEP, HALF)


def body(site_blocks, row_lengths, column_lengths, joining, owner_slots, next_blocks):
    sector_count, states, row_count, breadth = site_blocks.shape
    slots, local_columns = next_blocks.shape[:2]
    n_row = lax.axis_size("row")
    n_all = n_row * lax.axis_size("grp")
    both = ("grp", "row")
    quarters = n_row // slots
    piece_columns = local_columns // quarters
    tables = (
        row_lengths.reshape(1, -1),
        column_lengths.reshape(1, -1),
        joining.T,
        owner_slots.reshape(1, -1),
    )
    arrays = (
        site_blocks.reshape(n_row, row_count, breadth),
        next_blocks.reshape(n_row, piece_columns, breadth),
    ) + tables
    sent, rows_line, columns_line, joins, owner_line = pl.pallas_call(
        gather_kernel,
        out_shape=(
            jax.ShapeDtypeStruct((n_row, row_count + piece_columns, breadth), jnp.float32),
        )
        + tuple(jax.ShapeDtypeStruct(t.shape, t.dtype) for t in tables),
        in_specs=[HBM] * 6,
        out_specs=(VMEM,) * 5,
        scratch_shapes=[pltpu.SemaphoreType.DMA((6,))],
        compiler_params=PARAMS,
        name="gather",
    )(*(pltpu.with_memory_space_constraint(x, pltpu.HBM) for x in arrays))

    def swap(x):
        slots_of = x.reshape(n_all, 1, SLOT * HALF)
        return lax.all_to_all(slots_of, both, 0, 0, tiled=True).reshape(x.shape)

    data = lax.all_to_all(sent, "row", 0, 0, tiled=True)
    gram, meta, live, join_row, join_col, owner_col = pl.pallas_call(
        gram_kernel,
        out_shape=(
            jax.ShapeDtypeStruct((n_all * SLOT, HALF), jnp.float32),
            jax.ShapeDtypeStruct((2,), jnp.int32),
            jax.ShapeDtypeStruct((2, HALF), jnp.float32),
            jax.ShapeDtypeStruct((1, n_all), jnp.float32),
            jax.ShapeDtypeStruct((n_all, 1), jnp.float32),
            jax.ShapeDtypeStruct((n_all, 1), jnp.float32),
        ),
        in_specs=[SMEM, SMEM, SMEM, SMEM, VMEM, VMEM, VMEM, VMEM],
        out_specs=(VMEM, SMEM, VMEM, VMEM, VMEM, VMEM),
        compiler_params=PARAMS,
        name="gram",
    )(
        rows_line,
        columns_line,
        joins,
        owner_line,
        rows_line,
        joins,
        owner_line,
        data,
    )
    pieces = swap(gram)
    rows = pl.pallas_call(
        combine_kernel,
        out_shape=jax.ShapeDtypeStruct((n_all * SLOT, HALF), jnp.float32),
        in_specs=[SMEM, VMEM, VMEM, VMEM, VMEM],
        out_specs=VMEM,
        compiler_params=PARAMS,
        name="combine",
    )(meta, join_row, join_col, owner_col, pieces)
    grams = swap(rows)
    entries = float(n_row * local_columns * breadth * slots * lax.axis_size("grp"))
    result = pl.pallas_call(
        functools.partial(apply_kernel, entries),
        out_shape=jax.ShapeDtypeStruct(sent.shape, jnp.float32),
        in_specs=[SMEM, VMEM, VMEM, VMEM],
        out_specs=VMEM,
        scratch_shapes=[
            pltpu.VMEM((HALF, 2 * HALF), jnp.float32),
            pltpu.VMEM((HALF, 2 * HALF), jnp.float32),
            pltpu.VMEM((HALF, 4 * HALF), jnp.float32),
            pltpu.VMEM((2 * STEP, 2 * HALF), jnp.float32),
        ],
        compiler_params=PARAMS,
        name="factor_apply",
    )(meta, live, data, grams)
    back = lax.all_to_all(result, "row", 0, 0, tiled=True)
    canonical, next_site = pl.pallas_call(
        scatter_kernel,
        out_shape=(
            jax.ShapeDtypeStruct((n_row, row_count, breadth), jnp.float32),
            jax.ShapeDtypeStruct((n_row, piece_columns, breadth), jnp.float32),
        ),
        in_specs=[VMEM],
        out_specs=(HBM, HBM),
        scratch_shapes=[pltpu.SemaphoreType.DMA((2,))],
        compiler_params=PARAMS,
        name="scatter",
    )(back)
    canonical = canonical.reshape(site_blocks.shape)
    next_site = next_site.reshape(next_blocks.shape)
    return (canonical, next_site)


def solution(mesh):
    in_specs = (P("grp", None, "row", None), P(), P(), P(), P(), P("grp", "row", None))
    out_specs = (P("grp", None, "row", None), P("grp", "row", None))
    return jax.shard_map(body, mesh=mesh, in_specs=in_specs, out_specs=out_specs, check_vma=False)
```
